512 devices in a mesh: dp: 32 (over y, x, core), seq: 16 (over z).
Axes of the slice: x: 4, y: 4, z: 16, core: 2. Of those that a mesh axis runs over, the one named last changes fastest.
Arguments:
- tokens: bfloat16 [64, 4096, 768], P('dp', 'seq'), may hold values from -6 to 6
- norm_gain: float32 [768], replicated, may hold values from 0.1 to 1.9
- dilated_weight: bfloat16 [3, 768, 384], P(None, None, 'seq'), may hold values from -0.125 to 0.125
- output_weight: bfloat16 [384, 768], P(None, 'seq'), may hold values from -0.3125 to 0.3125
- cotangent: bfloat16 [64, 4096, 768], P('dp', 'seq'), may hold values from -6 to 6
Outputs:
- block_output: bfloat16 [64, 4096, 768], P('dp', 'seq')
- token_input_gradient: bfloat16 [64, 4096, 768], P('dp', 'seq')
- dilated_gradient: float32 [3, 768, 384], P(None, None, 'seq')
- output_gradient: float32 [384, 768], P(None, 'seq')
- gain_gradient: float32 [768], P('seq')
The draws below stay inside these ranges and needn't reach their ends.
All inputs are finite; a program needn't handle non-finite values.
Results may differ from the reference program's by a relative error of at most 0.017.
Values may be sent and summed in bfloat16 or wider, within the bound.
No kernel may reach another device: no remote copies, remote signals or barrier semaphores. Data moves between devices by JAX's collectives and lax.ppermute only.
A program may use at most 64 MiB of HBM per device.

```python
import jax
import jax.numpy as jnp
from jax import lax

TOWER_CHANNELS = 768
CH = 384
DILATION_STEP = 64
SEQ_DP = 2
SEQUENCE_COUNT = 64
SEQUENCE_BINS = 4096
N_DP = 32


def block_scale(stream_key, extent, split, low, largest):
    def one(dim, blocks):
        steps = jax.random.uniform(jax.random.fold_in(jax.random.fold_in(stream_key, 6), dim), (blocks,), jnp.float32, low / len(split), largest / len(split))
        return jnp.repeat(jnp.exp(steps), extent[dim] // blocks).reshape((-1,) + (1,) * (len(extent) - dim - 1))

    factor_of = one(*split[0])
    for cut in split[1:]:
        factor_of = factor_of * one(*cut)
    return factor_of


def normal_values(rng, shape, scale, bound, shards=(), kind=jnp.bfloat16):
    result = scale * jax.random.normal(rng, shape, jnp.float32)
    if shards:
        result = result * block_scale(rng, shape, shards, -0.22, 0.18)
    return jnp.clip(result, -bound, bound).astype(kind)


def setup_inputs(seed: int = 0) -> dict:
    key_of = jax.random.split(jax.random.key(seed), 6)
    return {
        "tokens": normal_values(key_of[0], (SEQUENCE_COUNT, SEQUENCE_BINS, TOWER_CHANNELS), 1.0, 6.0, ((0, 32), (1, 16))),
        "norm_gain": jnp.clip(1.0 + 0.18 * jax.random.normal(key_of[1], (TOWER_CHANNELS,), jnp.float32), 0.1, 1.9),
        "dilated_weight": normal_values(key_of[2], (3, TOWER_CHANNELS, CH), (3 * TOWER_CHANNELS) ** -0.5, 0.125, ((2, 16),)),
        "output_weight": normal_values(key_of[3], (CH, TOWER_CHANNELS), CH ** -0.5, 0.3125, ((1, 16),)),
        "cotangent": normal_values(key_of[4], (SEQUENCE_COUNT, SEQUENCE_BINS, TOWER_CHANNELS), 1.0, 6.0, ((0, 32), (1, 16))),
    }


gelu_scale = 0.7978845608
cubic_term = 0.044715
epsilon = 1e-06

def activate(value):
    inner = jnp.tanh(gelu_scale * (value + cubic_term * value * value * value))
    return 0.5 * value * (1.0 + inner)

def derivative(value):
    inner = jnp.tanh(gelu_scale * (value + cubic_term * value * value * value))
    return 0.5 * (1.0 + inner) + 0.5 * value * (1.0 - inner * inner) * gelu_scale * (1.0 + 3.0 * cubic_term * value * value)

def local_shares(left, right):
    left_f = left.astype(jnp.float32)
    right_f = right.astype(jnp.float32)
    return jnp.einsum('blp,blq->pq', left_f, right_f)

def reference(tokens, norm_gain, dilated_weight, output_weight, cotangent):
    groups = tokens.reshape(N_DP, SEQ_DP, SEQUENCE_BINS, TOWER_CHANNELS)
    cot_groups = cotangent.reshape(N_DP, SEQ_DP, SEQUENCE_BINS, TOWER_CHANNELS)

    def one_group(loop_carry, pair):
        running_dilated, running_output, running_gain = loop_carry
        tok_in, cot_in = pair
        as_float = tok_in.astype(jnp.float32)
        inverse_rms = lax.rsqrt(lax.optimization_barrier(jnp.mean(as_float * as_float, axis=-1, keepdims=True)) + epsilon)
        normed = as_float * inverse_rms * norm_gain
        gelu_activated = activate(normed).astype(jnp.bfloat16)
        padded_input = jnp.pad(gelu_activated, ((0, 0), (DILATION_STEP, DILATION_STEP), (0, 0)))
        shifted_input = [padded_input[:, tap_index * DILATION_STEP:tap_index * DILATION_STEP + SEQUENCE_BINS] for tap_index in range(3)]
        dilated_sum = jnp.zeros((SEQ_DP * SEQUENCE_BINS, CH), jnp.float32)
        for tap_index in range(3):
            dilated_sum = dilated_sum + jnp.dot(shifted_input[tap_index].reshape(-1, TOWER_CHANNELS), dilated_weight[tap_index], preferred_element_type=jnp.float32)
        dilated_sum = dilated_sum.reshape(SEQ_DP, SEQUENCE_BINS, CH)
        hidden = activate(dilated_sum).astype(jnp.bfloat16)
        projected = jnp.dot(hidden.reshape(-1, CH), output_weight, preferred_element_type=jnp.float32)
        residual_output = (as_float + projected.reshape(SEQ_DP, SEQUENCE_BINS, TOWER_CHANNELS)).astype(jnp.bfloat16)
        cot_rows = cot_in.reshape(-1, TOWER_CHANNELS)
        hidden_cot = jnp.dot(cot_rows, output_weight.T, preferred_element_type=jnp.float32).astype(jnp.bfloat16).reshape(SEQ_DP, SEQUENCE_BINS, CH)
        cotangent_sum = (hidden_cot.astype(jnp.float32) * derivative(dilated_sum)).astype(jnp.bfloat16)
        padded_cotangent = jnp.pad(cotangent_sum, ((0, 0), (DILATION_STEP, DILATION_STEP), (0, 0)))
        act_cot = jnp.zeros((SEQ_DP * SEQUENCE_BINS, TOWER_CHANNELS), jnp.float32)
        for tap_index in range(3):
            start_offset = (2 - tap_index) * DILATION_STEP
            act_cot = act_cot + jnp.dot(padded_cotangent[:, start_offset:start_offset + SEQUENCE_BINS].reshape(-1, CH), dilated_weight[tap_index].T, preferred_element_type=jnp.float32)
        act_cot = act_cot.astype(jnp.bfloat16).reshape(SEQ_DP, SEQUENCE_BINS, TOWER_CHANNELS)
        normed_cot = act_cot.astype(jnp.float32) * derivative(normed)
        scaled_cot = norm_gain * normed_cot
        token_cotangent = cot_in.astype(jnp.float32) + inverse_rms * scaled_cot - as_float * inverse_rms ** 3 * lax.optimization_barrier(jnp.mean(scaled_cot * as_float, axis=-1, keepdims=True))
        token_cotangent = token_cotangent.astype(jnp.bfloat16)
        dilated_piece = jnp.stack([local_shares(shifted_input[tap_index], cotangent_sum) for tap_index in range(3)])
        output_piece = local_shares(hidden, cot_in)
        gain_piece = lax.optimization_barrier(jnp.sum(normed_cot * as_float * inverse_rms, axis=(0, 1)))
        return ((running_dilated + dilated_piece, running_output + output_piece, running_gain + gain_piece), (residual_output, token_cotangent))
    start_carry = (jnp.zeros((3, TOWER_CHANNELS, CH), jnp.float32), jnp.zeros((CH, TOWER_CHANNELS), jnp.float32), jnp.zeros((TOWER_CHANNELS,), jnp.float32))
    reduced_totals, stacked = lax.scan(one_group, start_carry, (groups, cot_groups))
    running_dilated, running_output, running_gain = reduced_totals
    output_rows, token_gradient = stacked
    scale_factor = 1.0 / SEQUENCE_COUNT
    return (output_rows.reshape(SEQUENCE_COUNT, SEQUENCE_BINS, TOWER_CHANNELS), token_gradient.reshape(SEQUENCE_COUNT, SEQUENCE_BINS, TOWER_CHANNELS), running_dilated * scale_factor, running_output * scale_factor, running_gain * scale_factor)
```

```python
import jax
import jax.numpy as jnp
import numpy as np
from jax import lax
from jax.sharding import Mesh, PartitionSpec as P

DILATION_STEP = 64
gelu_scale = 0.7978845608
cubic_term = 0.044715
epsilon = 1e-06
bf16 = jnp.bfloat16
f32 = jnp.float32


def activate(value):
    inner = jnp.tanh(gelu_scale * (value + cubic_term * value * value * value))
    return 0.5 * value * (1.0 + inner)


def derivative(value):
    inner = jnp.tanh(gelu_scale * (value + cubic_term * value * value * value))
    return 0.5 * (1.0 + inner) + 0.5 * value * (1.0 - inner * inner) * gelu_scale * (
        1.0 + 3.0 * cubic_term * value * value
    )


def permutation(groups_outer, groups_inner, width):
    size = groups_outer * groups_inner * width
    order = np.arange(size).reshape(groups_inner, groups_outer, width).transpose(1, 0, 2).reshape(-1)
    matrix = np.zeros((size, size), np.float32)
    matrix[order, np.arange(size)] = 1.0
    return matrix


def on_device(tokens, norm_gain, dilated_weight, output_weight, cotangent):
    seqs, bins, channels = tokens.shape
    hidden_width = output_weight.shape[0]
    D = DILATION_STEP
    yx = ("y", "x")
    core = lax.axis_index("c")
    part = core * 16 + lax.axis_index(yx)
    lane_perm = jnp.asarray(permutation(4, 16, 6), bf16)
    row_perm = jnp.asarray(permutation(8, 16, 6), bf16)

    slice_d = (
        dilated_weight.transpose(0, 2, 1)
        .reshape(3, 4, 6, 2, 384)
        .transpose(1, 0, 3, 2, 4)
        .reshape(24, 6, 384)
    )
    slice_o = jnp.dot(output_weight.T, lane_perm, preferred_element_type=f32).astype(bf16)
    pieces = jnp.concatenate([slice_d, slice_o.reshape(8, 6, 384)])
    piece = lax.dynamic_index_in_dim(pieces, part, 0, keepdims=True)
    from_z = lax.all_to_all(jnp.broadcast_to(piece, (16, 6, 384)), "z", 0, 0)
    stacked = from_z.reshape(1, 96, 384)
    half = lax.all_to_all(jnp.broadcast_to(stacked, (16, 96, 384)), yx, 0, 0)
    other = lax.ppermute(half, "c", [(0, 1), (1, 0)])
    lower = jnp.where(core == 0, half, other)
    upper = jnp.where(core == 0, other, half)
    gathered = jnp.concatenate([lower, upper])
    taps = (
        gathered[:24].reshape(4, 3, 2, 96, 384).transpose(1, 0, 3, 2, 4).reshape(3, hidden_width, channels)
    )
    out_t = gathered[24:].reshape(channels, hidden_width)

    as_float = tokens.astype(f32)
    inverse_rms = lax.rsqrt(jnp.mean(as_float * as_float, axis=-1, keepdims=True) + epsilon)
    normed = as_float * inverse_rms * norm_gain
    activated = activate(normed).astype(bf16)
    cot_perm = jnp.einsum("snc,cd->snd", cotangent, row_perm, preferred_element_type=f32).astype(bf16)
    up = [(i, i + 1) for i in range(15)]
    down = [(i + 1, i) for i in range(15)]
    before = lax.ppermute(jnp.concatenate([activated[:, -2 * D :], cot_perm[:, -D:]], 1), "z", up)
    after = lax.ppermute(jnp.concatenate([activated[:, : 2 * D], cot_perm[:, :D]], 1), "z", down)
    act_ext = jnp.concatenate([before[:, : 2 * D], activated, after[:, : 2 * D]], 1)
    cot_ext = jnp.concatenate([before[:, 2 * D :], cot_perm, after[:, 2 * D :]], 1)

    ext = bins + 2 * D
    dilated_sum = sum(
        jnp.einsum("snc,hc->snh", act_ext[:, k * D : k * D + ext], taps[k], preferred_element_type=f32)
        for k in range(3)
    )
    hidden_cot = jnp.einsum("snc,ch->snh", cot_ext, out_t, preferred_element_type=f32).astype(bf16)
    sum_cot = (hidden_cot.astype(f32) * derivative(dilated_sum)).astype(bf16)
    hidden = activate(dilated_sum[:, D : D + bins]).astype(bf16)
    mine = sum_cot[:, D : D + bins]
    grad_d = jnp.stack(
        [
            jnp.einsum(
                "snh,snc->hc", mine, act_ext[:, (k + 1) * D : (k + 1) * D + bins], preferred_element_type=f32
            )
            for k in range(3)
        ]
    ).astype(bf16)
    grad_o = jnp.einsum("snc,snh->ch", cot_perm, hidden, preferred_element_type=f32).astype(bf16)
    grad = jnp.concatenate(
        [
            grad_d.reshape(3, 4, 96, 2, 384).transpose(1, 0, 3, 2, 4).reshape(24, 96, 384),
            grad_o.reshape(8, 96, 384),
        ]
    ).reshape(2, 16, 96, 384)
    keep = lax.dynamic_index_in_dim(grad, core, 0, keepdims=False)
    send = lax.dynamic_index_in_dim(grad, 1 - core, 0, keepdims=False)
    received = lax.ppermute(send, "c", [(0, 1), (1, 0)])
    chip = (keep.astype(f32) + received.astype(f32)).astype(bf16)
    plane = jnp.sum(lax.all_to_all(chip, yx, 0, 0).astype(f32), 0).astype(bf16).reshape(16, 6, 384)

    act_cot = sum(
        jnp.einsum("snh,hc->snc", sum_cot[:, (2 - k) * D : (2 - k) * D + bins], taps[k], preferred_element_type=f32)
        for k in range(3)
    )
    normed_cot = act_cot.astype(bf16).astype(f32) * derivative(normed)
    scaled_cot = norm_gain * normed_cot
    token_cotangent = (
        cotangent.astype(f32)
        + inverse_rms * scaled_cot
        - as_float * inverse_rms**3 * jnp.mean(scaled_cot * as_float, axis=-1, keepdims=True)
    ).astype(bf16)
    gain = jnp.sum(normed_cot * as_float * inverse_rms, axis=(0, 1)).reshape(16, 1, 48)
    out_nat = jnp.dot(row_perm, out_t, preferred_element_type=f32).astype(bf16)
    projected = jnp.einsum("snh,ch->snc", hidden, out_nat, preferred_element_type=f32)
    residual_output = (as_float + projected).astype(bf16)

    def with_gain(block, value):
        high = value.astype(bf16)
        low = (value - high.astype(f32)).astype(bf16)
        extra = jnp.concatenate([high, low], -2)
        extra = jnp.pad(extra, ((0, 0),) * (extra.ndim - 1) + ((0, 384 - 48),))
        return jnp.concatenate([block, extra], -2)

    over_z = lax.all_to_all(with_gain(plane, gain), "z", 0, 0).astype(f32)
    summed = jnp.sum(over_z, 0)
    gain_z = (summed[6:7] + summed[7:8])[:, :48]
    final = with_gain(summed[:6].astype(bf16), gain_z)
    spread = lax.all_to_all(jnp.broadcast_to(final[None], (32, 8, 384)), ("c", "y", "x"), 0, 0)
    scale = 1.0 / 64
    full = spread[:, :6]
    d_t = full[:24].reshape(4, 3, 2, 6, 384).transpose(1, 0, 3, 2, 4).reshape(3, 24, 768)
    o_t = jnp.einsum("ch,gh->cg", full[24:].reshape(48, 384), lane_perm, preferred_element_type=f32)
    gain_total = jnp.sum(spread[:, 6:, :48].astype(f32), axis=(0, 1))
    return (
        residual_output,
        token_cotangent,
        d_t.transpose(0, 2, 1).astype(f32) * scale,
        o_t.T * scale,
        gain_total * scale,
    )


def solution(mesh):
    fine = Mesh(mesh.devices.reshape(4, 4, 2, 16), ("y", "x", "c", "z"))
    dp = ("y", "x", "c")
    in_specs = (
        P(dp, "z", None),
        P(),
        P(None, None, "z"),
        P(None, "z"),
        P(dp, "z", None),
    )
    out_specs = (
        P(dp, "z", None),
        P(dp, "z", None),
        P(None, None, "z"),
        P(None, "z"),
        P("z"),
    )
    return jax.shard_map(on_device, mesh=fine, in_specs=in_specs, out_specs=out_specs, check_vma=False)
```

```python
import jax
import jax.numpy as jnp
import numpy as np
from jax import lax
from jax.sharding import Mesh, PartitionSpec as P

DILATION_STEP = 64
gelu_scale = 0.7978845608
cubic_term = 0.044715
epsilon = 1e-06
bf16 = jnp.bfloat16
f32 = jnp.float32


def activate(value):
    inner = jnp.tanh(gelu_scale * (value + cubic_term * value * value * value))
    return 0.5 * value * (1.0 + inner)


def derivative(value):
    inner = jnp.tanh(gelu_scale * (value + cubic_term * value * value * value))
    return 0.5 * (1.0 + inner) + 0.5 * value * (1.0 - inner * inner) * gelu_scale * (
        1.0 + 3.0 * cubic_term * value * value
    )


def permutation(groups_outer, groups_inner, width):
    size = groups_outer * groups_inner * width
    order = np.arange(size).reshape(groups_inner, groups_outer, width).transpose(1, 0, 2).reshape(-1)
    matrix = np.zeros((size, size), np.float32)
    matrix[order, np.arange(size)] = 1.0
    return matrix


def on_device(tokens, norm_gain, dilated_weight, output_weight, cotangent):
    seqs, bins, channels = tokens.shape
    hidden_width = output_weight.shape[0]
    D = DILATION_STEP
    yx = ("y", "x")
    core = lax.axis_index("c")
    part = core * 16 + lax.axis_index(yx)
    lane_perm = jnp.asarray(permutation(4, 16, 6), bf16)
    row_perm = jnp.asarray(permutation(8, 16, 6), bf16)

    as_float = tokens.astype(f32)
    inverse_rms = lax.rsqrt(jnp.mean(as_float * as_float, axis=-1, keepdims=True) + epsilon)
    normed = as_float * inverse_rms * norm_gain
    activated = activate(normed).astype(bf16)
    cot_perm = jnp.einsum("snc,cd->snd", cotangent, row_perm, preferred_element_type=f32).astype(bf16)
    up = [(i, i + 1) for i in range(15)]
    down = [(i + 1, i) for i in range(15)]
    before = lax.ppermute(jnp.concatenate([activated[:, -2 * D :], cot_perm[:, -D:]], 1), "z", up)
    after = lax.ppermute(jnp.concatenate([activated[:, : 2 * D], cot_perm[:, :D]], 1), "z", down)

    slice_d = (
        dilated_weight.transpose(0, 2, 1)
        .reshape(3, 4, 6, 2, 384)
        .transpose(1, 0, 3, 2, 4)
        .reshape(24, 6, 384)
    )
    slice_o = jnp.dot(output_weight.T, lane_perm, preferred_element_type=f32).astype(bf16)
    pieces = jnp.concatenate([slice_d, slice_o.reshape(8, 6, 384)])
    piece = lax.dynamic_index_in_dim(pieces, part, 0, keepdims=True)
    from_z = lax.all_to_all(jnp.broadcast_to(piece, (16, 6, 384)), "z", 0, 0)
    from_z, before, after = lax.optimization_barrier((from_z, before, after))
    stacked = from_z.reshape(1, 96, 384)
    half = lax.all_to_all(jnp.broadcast_to(stacked, (16, 96, 384)), yx, 0, 0)
    other = lax.ppermute(half, "c", [(0, 1), (1, 0)])
    lower = jnp.where(core == 0, half, other)
    upper = jnp.where(core == 0, other, half)
    gathered = jnp.concatenate([lower, upper])
    taps = (
        gathered[:24].reshape(4, 3, 2, 96, 384).transpose(1, 0, 3, 2, 4).reshape(3, hidden_width, channels)
    )
    out_t = gathered[24:].reshape(channels, hidden_width)

    act_ext = jnp.concatenate([before[:, : 2 * D], activated, after[:, : 2 * D]], 1)
    cot_ext = jnp.concatenate([before[:, 2 * D :], cot_perm, after[:, 2 * D :]], 1)

    ext = bins + 2 * D
    dilated_sum = sum(
        jnp.einsum("snc,hc->snh", act_ext[:, k * D : k * D + ext], taps[k], preferred_element_type=f32)
        for k in range(3)
    )
    hidden_cot = jnp.einsum("snc,ch->snh", cot_ext, out_t, preferred_element_type=f32).astype(bf16)
    sum_cot = (hidden_cot.astype(f32) * derivative(dilated_sum)).astype(bf16)
    hidden = activate(dilated_sum[:, D : D + bins]).astype(bf16)
    mine = sum_cot[:, D : D + bins]
    grad_d = jnp.stack(
        [
            jnp.einsum(
                "snh,snc->hc", mine, act_ext[:, (k + 1) * D : (k + 1) * D + bins], preferred_element_type=f32
            )
            for k in range(3)
        ]
    ).astype(bf16)
    grad_o = jnp.einsum("snc,snh->ch", cot_perm, hidden, preferred_element_type=f32).astype(bf16)
    grad = jnp.concatenate(
        [
            grad_d.reshape(3, 4, 96, 2, 384).transpose(1, 0, 3, 2, 4).reshape(24, 96, 384),
            grad_o.reshape(8, 96, 384),
        ]
    ).reshape(2, 16, 96, 384)
    keep = lax.dynamic_index_in_dim(grad, core, 0, keepdims=False)
    send = lax.dynamic_index_in_dim(grad, 1 - core, 0, keepdims=False)
    received = lax.ppermute(send, "c", [(0, 1), (1, 0)])
    chip = (keep.astype(f32) + received.astype(f32)).astype(bf16)
    plane = jnp.sum(lax.all_to_all(chip, yx, 0, 0).astype(f32), 0).astype(bf16).reshape(16, 6, 384)

    act_cot = sum(
        jnp.einsum("snh,hc->snc", sum_cot[:, (2 - k) * D : (2 - k) * D + bins], taps[k], preferred_element_type=f32)
        for k in range(3)
    )
    normed_cot = act_cot.astype(bf16).astype(f32) * derivative(normed)
    scaled_cot = norm_gain * normed_cot
    token_cotangent = (
        cotangent.astype(f32)
        + inverse_rms * scaled_cot
        - as_float * inverse_rms**3 * jnp.mean(scaled_cot * as_float, axis=-1, keepdims=True)
    ).astype(bf16)
    gain = jnp.sum(normed_cot * as_float * inverse_rms, axis=(0, 1)).reshape(16, 1, 48)
    out_nat = jnp.dot(row_perm, out_t, preferred_element_type=f32).astype(bf16)
    projected = jnp.einsum("snh,ch->snc", hidden, out_nat, preferred_element_type=f32)
    residual_output = (as_float + projected).astype(bf16)

    plane, gain, residual_output, token_cotangent = lax.optimization_barrier(
        (plane, gain, residual_output, token_cotangent)
    )

    def with_gain(block, value):
        high = value.astype(bf16)
        low = (value - high.astype(f32)).astype(bf16)
        extra = jnp.concatenate([high, low], -2)
        extra = jnp.pad(extra, ((0, 0),) * (extra.ndim - 1) + ((0, 384 - 48),))
        return jnp.concatenate([block, extra], -2)

    over_z = lax.all_to_all(with_gain(plane, gain), "z", 0, 0).astype(f32)
    summed = jnp.sum(over_z, 0)
    gain_z = (summed[6:7] + summed[7:8])[:, :48]
    final = with_gain(summed[:6].astype(bf16), gain_z)
    spread = lax.all_to_all(jnp.broadcast_to(final[None], (32, 8, 384)), ("c", "y", "x"), 0, 0)
    scale = 1.0 / 64
    full = spread[:, :6]
    d_t = full[:24].reshape(4, 3, 2, 6, 384).transpose(1, 0, 3, 2, 4).reshape(3, 24, 768)
    o_t = jnp.einsum("ch,gh->cg", full[24:].reshape(48, 384), lane_perm, preferred_element_type=f32)
    gain_total = jnp.sum(spread[:, 6:, :48].astype(f32), axis=(0, 1))
    return (
        residual_output,
        token_cotangent,
        d_t.transpose(0, 2, 1).astype(f32) * scale,
        o_t.T * scale,
        gain_total * scale,
    )


def solution(mesh):
    fine = Mesh(mesh.devices.reshape(4, 4, 2, 16), ("y", "x", "c", "z"))
    dp = ("y", "x", "c")
    in_specs = (
        P(dp, "z", None),
        P(),
        P(None, None, "z"),
        P(None, "z"),
        P(dp, "z", None),
    )
    out_specs = (
        P(dp, "z", None),
        P(dp, "z", None),
        P(None, None, "z"),
        P(None, "z"),
        P("z"),
    )
    return jax.shard_map(on_device, mesh=fine, in_specs=in_specs, out_specs=out_specs, check_vma=False)
```

```python
import jax
import jax.numpy as jnp
import numpy as np
from jax import lax
from jax.experimental import pallas as pl
from jax.experimental.pallas import tpu as pltpu
from jax.sharding import Mesh, PartitionSpec as P

STEP = 64
SEQS = 2
BINS = 256
CHANNELS = 768
HIDDEN = 384
EXT = BINS + 2 * STEP
gelu_scale = 0.7978845608
cubic_term = 0.044715
epsilon = 1e-06
bf16 = jnp.bfloat16
f32 = jnp.float32
HBM = pl.BlockSpec(memory_space=pl.ANY)
SMEM = pl.BlockSpec(memory_space=pltpu.SMEM)
VMEM = pl.BlockSpec(memory_space=pltpu.VMEM)
PARAMS = pltpu.CompilerParams(vmem_limit_bytes=48 * 1024 * 1024)


def permutation(outer, inner, width):
    size = outer * inner * width
    order = np.arange(size).reshape(inner, outer, width).transpose(1, 0, 2).reshape(-1)
    matrix = np.zeros((size, size), np.float32)
    matrix[order, np.arange(size)] = 1.0
    return matrix


def dot(a, b, ca, cb):
    return lax.dot_general(a, b, (((ca,), (cb,)), ((), ())), preferred_element_type=f32)


def tanh_of(v):
    return jnp.tanh(gelu_scale * (v + cubic_term * v * v * v))


def activate(v, t):
    return 0.5 * v * (1.0 + t)


def derivative(v, t):
    return 0.5 * (1.0 + t) + 0.5 * v * (1.0 - t * t) * gelu_scale * (1.0 + 3.0 * cubic_term * v * v)


def inverse_rms_of(v):
    return lax.rsqrt(jnp.mean(v * v, axis=-1, keepdims=True) + epsilon)


def piece_kernel(part, taps, proj, perm, out, pieces):
    for k in range(3):
        tap = taps[k].astype(f32)
        for q in range(4):
            for half in range(2):
                pieces[(q * 3 + k) * 2 + half, 0:6] = tap[6 * q : 6 * q + 6, half * 384 : half * 384 + 384]
    rows = dot(proj[...], perm[...], 1, 0)
    for u in range(8):
        pieces[24 + u, 0:6] = rows[6 * u : 6 * u + 6]
    pieces[:, 6:8] = jnp.zeros((32, 2, 384), f32)
    own = pieces[part[0]].astype(bf16)
    for z in range(16):
        out[z] = own


def stack_kernel(given, out, rows, packed, sems):
    for z in range(16):
        rows[6 * z : 6 * z + 6] = given[z].astype(f32)[0:6]
    packed[...] = rows[...].astype(bf16)
    copies = [pltpu.make_async_copy(packed, out.at[i], sems.at[i]) for i in range(16)]
    for c in copies:
        c.start()
    for c in copies:
        c.wait()


def norm_kernel(tokens, gain, cot, perm, activated, cot_perm, up, down):
    v = tokens[0].astype(f32)
    normed = v * inverse_rms_of(v) * gain[...]
    a = activate(normed, tanh_of(normed)).astype(bf16)
    c = dot(cot[0], perm[...], 1, 0).astype(bf16)
    activated[0] = a
    cot_perm[0] = c
    up[0, 0 : 2 * STEP] = a[BINS - 2 * STEP :]
    up[0, 2 * STEP :] = c[BINS - STEP :]
    down[0, 0 : 2 * STEP] = a[: 2 * STEP]
    down[0, 2 * STEP :] = c[:STEP]


def weight_copies(core, mine, other, taps, proj, sems, act):
    for here in range(2):

        @pl.when(core[0] == here)
        def _(here=here):
            for p in range(32):
                source = (mine if p // 16 == here else other).at[p % 16]
                if p < 24:
                    q, k, half = p // 6, p % 6 // 2, p % 2
                    target = taps.at[k, 96 * q : 96 * q + 96, 384 * half : 384 * half + 384]
                else:
                    target = proj.at[96 * (p - 24) : 96 * (p - 24) + 96]
                copy = pltpu.make_async_copy(source, target, sems.at[p])
                copy.start() if act else copy.wait()


def main_kernel(
    core, mine, other, activated, cot_perm, before, after,
    keep, send, sum_cot_out, hidden_out,
    taps, proj, act, cot, sum_cot, hidden, grad, wsems, sems,
):
    weight_copies(core, mine, other, taps, proj, wsems, True)
    halo, own = 2 * STEP, BINS
    loads = [
        (before.at[:, 0:halo], act.at[:, 0:halo]),
        (activated, act.at[:, halo : halo + own]),
        (after.at[:, 0:halo], act.at[:, halo + own :]),
        (before.at[:, halo:], cot.at[:, 0:STEP]),
        (cot_perm, cot.at[:, STEP : STEP + own]),
        (after.at[:, halo:], cot.at[:, STEP + own :]),
    ]
    loads = [pltpu.make_async_copy(a, b, sems.at[i]) for i, (a, b) in enumerate(loads)]
    for c in loads:
        c.start()
    for c in loads:
        c.wait()
    weight_copies(core, mine, other, taps, proj, wsems, False)
    for s in range(SEQS):
        total = dot(act[s, 0:EXT], taps[0], 1, 1)
        total += dot(act[s, STEP : STEP + EXT], taps[1], 1, 1)
        total += dot(act[s, 2 * STEP : 2 * STEP + EXT], taps[2], 1, 1)
        hidden_cot = dot(cot[s], proj[...], 1, 0).astype(bf16).astype(f32)
        t = tanh_of(total)
        hidden[s] = activate(total, t)[STEP : STEP + own].astype(bf16)
        sum_cot[s] = (hidden_cot * derivative(total, t)).astype(bf16)
    saves = [
        pltpu.make_async_copy(sum_cot, sum_cot_out, sems.at[6]),
        pltpu.make_async_copy(hidden, hidden_out, sems.at[7]),
    ]
    for c in saves:
        c.start()
    centre = jnp.concatenate([sum_cot[s, STEP : STEP + own] for s in range(SEQS)])
    for k in range(3):
        rows = jnp.concatenate([act[s, STEP * (k + 1) : STEP * (k + 1) + own] for s in range(SEQS)])
        g = dot(centre, rows, 0, 0).astype(bf16)
        for q in range(4):
            for half in range(2):
                grad[(q * 3 + k) * 2 + half] = g[96 * q : 96 * q + 96, 384 * half : 384 * half + 384]
    rows = jnp.concatenate([cot[s, STEP : STEP + own] for s in range(SEQS)])
    g = dot(rows, jnp.concatenate([hidden[s] for s in range(SEQS)]), 0, 0).astype(bf16)
    for u in range(8):
        grad[24 + u] = g[96 * u : 96 * u + 96]
    saves += [
        pltpu.make_async_copy(grad.at[pl.ds(16 * core[0], 16)], keep, sems.at[8]),
        pltpu.make_async_copy(grad.at[pl.ds(16 - 16 * core[0], 16)], send, sems.at[9]),
    ]
    for c in saves[2:]:
        c.start()
    for c in saves:
        c.wait()


def pair_kernel(a, b, out):
    out[...] = (a[...].astype(f32) + b[...].astype(f32)).astype(bf16)


def tail_kernel(
    core, mine, other, sum_cot, hidden, tokens, gain, cot, perm,
    block_output, token_gradient, gain_rows,
    taps, proj, wsems,
):
    weight_copies(core, mine, other, taps, proj, wsems, True)
    weight_copies(core, mine, other, taps, proj, wsems, False)
    natural = dot(perm[...], proj[...], 1, 0).astype(bf16)
    gain_row = gain[...]
    gain_sum = jnp.zeros((1, CHANNELS), f32)
    for s in range(SEQS):
        v = tokens[s].astype(f32)
        block_output[s] = (v + dot(hidden[s], natural, 1, 1)).astype(bf16)
        total = dot(sum_cot[s, 2 * STEP : 2 * STEP + BINS], taps[0], 1, 0)
        total += dot(sum_cot[s, STEP : STEP + BINS], taps[1], 1, 0)
        total += dot(sum_cot[s, 0:BINS], taps[2], 1, 0)
        inverse_rms = inverse_rms_of(v)
        normed = v * inverse_rms * gain_row
        normed_cot = total.astype(bf16).astype(f32) * derivative(normed, tanh_of(normed))
        scaled_cot = gain_row * normed_cot
        mean = jnp.mean(scaled_cot * v, axis=-1, keepdims=True)
        token_gradient[s] = (
            cot[s].astype(f32) + inverse_rms * scaled_cot - v * (inverse_rms * inverse_rms * inverse_rms) * mean
        ).astype(bf16)
        gain_sum += jnp.sum(normed_cot * v * inverse_rms, axis=0, keepdims=True)
    gain_rows[...] = jnp.zeros((16, 384), f32)
    for z in range(16):
        gain_rows[z : z + 1, 0:48] = gain_sum[:, 48 * z : 48 * z + 48]


def split_high_low(v):
    high = v.astype(bf16).astype(f32)
    return high, v - high


def plane_kernel(given, gain_rows, out, rows):
    total = given[0].astype(f32)
    for i in range(1, 16):
        total += given[i].astype(f32)
    rows[...] = total
    for z in range(16):
        high, low = split_high_low(gain_rows[z : z + 1])
        out[z] = jnp.concatenate([rows[6 * z : 6 * z + 6], high, low]).astype(bf16)


def column_kernel(given, out):
    total = given[0].astype(f32)
    for z in range(1, 16):
        total += given[z].astype(f32)
    high, low = split_high_low(total[6:7] + total[7:8])
    block = jnp.concatenate([total[0:6], high, low]).astype(bf16)
    for i in range(32):
        out[i] = block


def final_kernel(given, perm, taps, proj, gain, rows):
    scale = 1.0 / 64
    for q in range(4):
        for k in range(3):
            for half in range(2):
                block = given[(q * 3 + k) * 2 + half].astype(f32)
                taps[k, 6 * q : 6 * q + 6, 384 * half : 384 * half + 384] = block[0:6] * scale
    for u in range(8):
        rows[6 * u : 6 * u + 6] = given[24 + u].astype(f32)[0:6]
    proj[...] = dot(rows[...].astype(bf16), perm[...], 1, 1) * scale
    total = given[0].astype(f32)
    for i in range(1, 32):
        total += given[i].astype(f32)
    gain[...] = (total[6:7] + total[7:8])[:, 0:128] * scale


def call(kernel, out, ins, outs, name, scratch=(), **more):
    return pl.pallas_call(
        kernel,
        out_shape=out,
        in_specs=ins,
        out_specs=outs,
        scratch_shapes=scratch,
        compiler_params=PARAMS,
        name=name,
        **more,
    )


def shape(dims, kind):
    return jax.ShapeDtypeStruct(dims, kind)


HALF = shape((16, 96, 384), bf16)
ROWS = shape((SEQS, BINS, CHANNELS), bf16)
WEIGHTS = [pltpu.VMEM((3, HIDDEN, CHANNELS), bf16), pltpu.VMEM((CHANNELS, HIDDEN), bf16)]


def make_piece(part, taps, proj, perm):
    return call(
        piece_kernel, shape((16, 8, 384), bf16), [SMEM] + [VMEM] * 3, VMEM, "piece", [pltpu.VMEM((32, 8, 384), f32)]
    )(part, taps, proj, perm)


def make_stack(given):
    scratch = [pltpu.VMEM((96, 384), f32), pltpu.VMEM((96, 384), bf16), pltpu.SemaphoreType.DMA((16,))]
    return call(stack_kernel, HALF, [VMEM], HBM, "stack", scratch)(given)


def make_norm(tokens, gain, cot, perm):
    block = pl.BlockSpec((1, BINS, CHANNELS), lambda s: (s, 0, 0))
    edge = pl.BlockSpec((1, 3 * STEP, CHANNELS), lambda s: (s, 0, 0))
    edge_shape = shape((SEQS, 3 * STEP, CHANNELS), bf16)
    return call(
        norm_kernel,
        [ROWS, ROWS, edge_shape, edge_shape],
        [
            block,
            pl.BlockSpec((1, CHANNELS), lambda s: (0, 0)),
            block,
            pl.BlockSpec((CHANNELS, CHANNELS), lambda s: (0, 0)),
        ],
        [block, block, edge, edge],
        "norm",
        grid=(SEQS,),
    )(tokens, gain, cot, perm)


def make_main(core, mine, other, activated, cot_perm, before, after):
    sum_cot = (SEQS, EXT, HIDDEN)
    hidden = (SEQS, BINS, HIDDEN)
    return call(
        main_kernel,
        [HALF, HALF, shape(sum_cot, bf16), shape(hidden, bf16)],
        [SMEM] + [HBM] * 6,
        [HBM] * 4,
        "main",
        WEIGHTS
        + [
            pltpu.VMEM((SEQS, BINS + 4 * STEP, CHANNELS), bf16),
            pltpu.VMEM((SEQS, EXT, CHANNELS), bf16),
            pltpu.VMEM(sum_cot, bf16),
            pltpu.VMEM(hidden, bf16),
            pltpu.VMEM((32, 96, 384), bf16),
            pltpu.SemaphoreType.DMA((32,)),
            pltpu.SemaphoreType.DMA((10,)),
        ],
    )(core, mine, other, activated, cot_perm, before, after)


def make_pair(a, b):
    block = pl.BlockSpec((4, 96, 384), lambda i: (i, 0, 0))
    return call(pair_kernel, HALF, [block, block], block, "pair", grid=(4,))(a, b)


def make_tail(core, mine, other, sum_cot, hidden, tokens, gain, cot, perm):
    return call(
        tail_kernel,
        [ROWS, ROWS, shape((16, 384), f32)],
        [SMEM, HBM, HBM] + [VMEM] * 6,
        [VMEM] * 3,
        "tail",
        WEIGHTS + [pltpu.SemaphoreType.DMA((32,))],
    )(core, mine, other, sum_cot, hidden, tokens, gain, cot, perm)


def make_plane(given, gain_rows):
    return call(
        plane_kernel, shape((16, 8, 384), bf16), [VMEM] * 2, VMEM, "plane", [pltpu.VMEM((96, 384), f32)]
    )(given, gain_rows)


def make_column(given):
    return call(column_kernel, shape((32, 8, 384), bf16), [VMEM], VMEM, "column")(given)


def make_final(given, perm):
    return call(
        final_kernel,
        [shape((3, 24, CHANNELS), f32), shape((48, 384), f32), shape((1, 128), f32)],
        [VMEM] * 2,
        [VMEM] * 3,
        "final",
        [pltpu.VMEM((48, 384), f32)],
    )(given, perm)


def on_device(tokens, norm_gain, dilated_weight, output_weight, cotangent):
    yx = ("y", "x")
    swap = [(0, 1), (1, 0)]
    core = lax.axis_index("c").reshape(1)
    part = core * 16 + lax.axis_index(yx)
    lane_perm = jnp.asarray(permutation(4, 16, 6), bf16)
    row_perm = jnp.asarray(permutation(8, 16, 6), bf16)
    gain_row = norm_gain.reshape(1, CHANNELS)

    activated, cot_perm, up, down = make_norm(tokens, gain_row, cotangent, row_perm)
    before = lax.ppermute(up, "z", [(i, i + 1) for i in range(15)])
    after = lax.ppermute(down, "z", [(i + 1, i) for i in range(15)])

    piece = make_piece(part, dilated_weight.transpose(0, 2, 1), output_weight.T, lane_perm)
    from_z = lax.all_to_all(piece, "z", 0, 0)
    from_z, before, after = lax.optimization_barrier((from_z, before, after))
    mine = lax.all_to_all(make_stack(from_z), yx, 0, 0)
    other = lax.ppermute(mine, "c", swap)

    keep, send, sum_cot, hidden = make_main(core, mine, other, activated, cot_perm, before, after)
    received = lax.ppermute(send, "c", swap)
    plane = lax.all_to_all(make_pair(keep, received), yx, 0, 0)
    residual_output, token_cotangent, gain_rows = make_tail(
        core, mine, other, sum_cot, hidden, tokens, gain_row, cotangent, row_perm
    )
    column = lax.all_to_all(make_plane(plane, gain_rows), "z", 0, 0)
    spread = lax.all_to_all(make_column(column), ("c", "y", "x"), 0, 0)
    taps, proj, gain = make_final(spread, lane_perm)
    return residual_output, token_cotangent, taps.transpose(0, 2, 1), proj.T, gain[0, :48]


def solution(mesh):
    fine = Mesh(mesh.devices.reshape(4, 4, 2, 16), ("y", "x", "c", "z"))
    dp = ("y", "x", "c")
    rows = P(dp, "z", None)
    in_specs = (rows, P(), P(None, None, "z"), P(None, "z"), rows)
    out_specs = (rows, rows, P(None, None, "z"), P(None, "z"), P("z"))
    return jax.shard_map(on_device, mesh=fine, in_specs=in_specs, out_specs=out_specs, check_vma=False)
```

```python
import jax
import jax.numpy as jnp
import numpy as np
from jax import lax
from jax.experimental import pallas as pl
from jax.experimental.pallas import tpu as pltpu
from jax.sharding import Mesh, PartitionSpec as P

STEP = 64
SEQS = 2
BINS = 256
CHANNELS = 768
HIDDEN = 384
EXT = BINS + 2 * STEP
gelu_scale = 0.7978845608
cubic_term = 0.044715
epsilon = 1e-06
bf16 = jnp.bfloat16
f32 = jnp.float32
HBM = pl.BlockSpec(memory_space=pl.ANY)
SMEM = pl.BlockSpec(memory_space=pltpu.SMEM)
VMEM = pl.BlockSpec(memory_space=pltpu.VMEM)
FAR = pl.BlockSpec(memory_space=pltpu.HBM)
MB = 1024 * 1024


def permutation(outer, inner, width):
    size = outer * inner * width
    order = np.arange(size).reshape(inner, outer, width).transpose(1, 0, 2).reshape(-1)
    matrix = np.zeros((size, size), np.float32)
    matrix[order, np.arange(size)] = 1.0
    return matrix


def dot(a, b, ca, cb):
    return lax.dot_general(a, b, (((ca,), (cb,)), ((), ())), preferred_element_type=f32)


def tanh_of(v):
    return jnp.tanh(gelu_scale * (v + cubic_term * v * v * v))


def activate(v, t):
    return 0.5 * v * (1.0 + t)


def derivative(v, t):
    return 0.5 * (1.0 + t) + 0.5 * v * (1.0 - t * t) * gelu_scale * (1.0 + 3.0 * cubic_term * v * v)


def inverse_rms_of(v):
    return lax.rsqrt(jnp.mean(v * v, axis=-1, keepdims=True) + epsilon)


def piece_kernel(part, taps, proj, perm, out, pieces):
    for k in range(3):
        tap = taps[k].astype(f32)
        for q in range(4):
            for half in range(2):
                pieces[(q * 3 + k) * 2 + half, 0:6] = tap[6 * q : 6 * q + 6, half * 384 : half * 384 + 384]
    rows = dot(proj[...], perm[...], 1, 0)
    for u in range(8):
        pieces[24 + u, 0:6] = rows[6 * u : 6 * u + 6]
    pieces[:, 6:8] = jnp.zeros((32, 2, 384), f32)
    own = pieces[part[0]].astype(bf16)
    for z in range(16):
        out[z] = own


def stack_kernel(given, out, rows):
    for z in range(16):
        rows[6 * z : 6 * z + 6] = given[z].astype(f32)[0:6]
    packed = rows[...].astype(bf16)
    for i in range(16):
        out[i] = packed


def run(pairs, sems):
    copies = [pltpu.make_async_copy(a, b, sems.at[i]) for i, (a, b) in enumerate(pairs)]
    for c in copies:
        c.start()
    return copies


def norm_kernel(tokens, gain_in, cot, up, down, rows, gain, sems):
    loads = [(tokens.at[s], rows.at[s]) for s in range(SEQS)]
    loads += [
        (gain_in, gain),
        (cot.at[:, BINS - STEP :], up.at[:, 2 * STEP :]),
        (cot.at[:, 0:STEP], down.at[:, 2 * STEP :]),
    ]
    loads = run(loads, sems)
    loads[SEQS].wait()
    gain_row = gain[...].reshape(1, CHANNELS)
    for s in range(SEQS):
        loads[s].wait()
        v = rows[s].astype(f32)
        normed = v * inverse_rms_of(v) * gain_row
        a = activate(normed, tanh_of(normed)).astype(bf16)
        up[s, 0 : 2 * STEP] = a[BINS - 2 * STEP :]
        down[s, 0 : 2 * STEP] = a[: 2 * STEP]
    for c in loads[SEQS + 1 :]:
        c.wait()


def ready_kernel(
    tokens, gain, cot, perm, up, down, before, after,
    act, cot_perm, slope,
    rows, cots, matrix, sems,
):
    loads = [(cot, cots), (perm, matrix), (tokens, rows)]
    loads = run(loads, sems)
    half = 2 * STEP
    act[:, 0:half] = before[:, 0:half]
    act[:, half : 2 * half] = down[:, 0:half]
    act[:, 2 * half : 3 * half] = up[:, 0:half]
    act[:, 3 * half :] = after[:, 0:half]
    for c in loads:
        c.wait()
    order = matrix[...]
    gain_row = gain[...].reshape(1, CHANNELS)
    for s in range(SEQS):
        cot_perm[s, STEP : STEP + BINS] = dot(cots[s], order, 1, 0).astype(bf16)
        edges = dot(jnp.concatenate([before[s, half:], after[s, half:]]), order, 1, 0).astype(bf16)
        cot_perm[s, 0:STEP] = edges[0:STEP]
        cot_perm[s, STEP + BINS :] = edges[STEP:]
        v = rows[s].astype(f32)
        normed = v * inverse_rms_of(v) * gain_row
        slope[s] = derivative(normed, tanh_of(normed))


def weight_copies(core, mine, other, taps, proj, sems, act):
    for here in range(2):

        @pl.when(core[0] == here)
        def _(here=here):
            for p in range(32):
                source = (mine if p // 16 == here else other).at[p % 16]
                if p < 24:
                    q, k, half = p // 6, p % 6 // 2, p % 2
                    target = taps.at[k, 96 * q : 96 * q + 96, 384 * half : 384 * half + 384]
                else:
                    target = proj.at[96 * (p - 24) : 96 * (p - 24) + 96]
                copy = pltpu.make_async_copy(source, target, sems.at[p])
                copy.start() if act else copy.wait()


def main_kernel(
    core, mine, other, act, cot,
    keep, send, sum_cot, hidden, taps, proj,
    grad, wsems, sems,
):
    own = BINS
    weight_copies(core, mine, other, taps, proj, wsems, True)
    weight_copies(core, mine, other, taps, proj, wsems, False)
    for s in range(SEQS):
        total = dot(act[s, 0:EXT], taps[0], 1, 1)
        total += dot(act[s, STEP : STEP + EXT], taps[1], 1, 1)
        total += dot(act[s, 2 * STEP : 2 * STEP + EXT], taps[2], 1, 1)
        hidden_cot = dot(cot[s], proj[...], 1, 0).astype(bf16).astype(f32)
        t = tanh_of(total)
        hidden[s] = activate(total, t)[STEP : STEP + own].astype(bf16)
        sum_cot[s] = (hidden_cot * derivative(total, t)).astype(bf16)
    centre = jnp.concatenate([sum_cot[s, STEP : STEP + own] for s in range(SEQS)])
    for k in range(3):
        rows = jnp.concatenate([act[s, STEP * (k + 1) : STEP * (k + 1) + own] for s in range(SEQS)])
        g = dot(centre, rows, 0, 0).astype(bf16)
        for q in range(4):
            for half in range(2):
                grad[(q * 3 + k) * 2 + half] = g[96 * q : 96 * q + 96, 384 * half : 384 * half + 384]
    rows = jnp.concatenate([cot[s, STEP : STEP + own] for s in range(SEQS)])
    g = dot(rows, jnp.concatenate([hidden[s] for s in range(SEQS)]), 0, 0).astype(bf16)
    for u in range(8):
        grad[24 + u] = g[96 * u : 96 * u + 96]
    saves = [
        (grad.at[pl.ds(16 * core[0], 16)], keep),
        (grad.at[pl.ds(16 - 16 * core[0], 16)], send),
    ]
    for c in run(saves, sems):
        c.wait()


def pair_kernel(a, b, out):
    out[...] = (a[...].astype(f32) + b[...].astype(f32)).astype(bf16)


def tail_kernel(
    taps, proj, sum_cot, hidden, slope, tokens, gain, cot, perm,
    block_output, token_gradient, gain_rows,
    rows, cots, matrix, result, sems, out_sems,
):
    loads = run([(tokens, rows), (cot, cots), (perm, matrix)], sems)
    for c in loads:
        c.wait()
    natural = dot(matrix[...], proj[...], 1, 0).astype(bf16)
    gain_row = gain[...].reshape(1, CHANNELS)
    gain_sum = jnp.zeros((1, CHANNELS), f32)
    saves = []
    for s in range(SEQS):
        v = rows[s].astype(f32)
        result[0, s] = (v + dot(hidden[s], natural, 1, 1)).astype(bf16)
        total = dot(sum_cot[s, 2 * STEP : 2 * STEP + BINS], taps[0], 1, 0)
        total += dot(sum_cot[s, STEP : STEP + BINS], taps[1], 1, 0)
        total += dot(sum_cot[s, 0:BINS], taps[2], 1, 0)
        inverse_rms = inverse_rms_of(v)
        normed_cot = total.astype(bf16).astype(f32) * slope[s]
        scaled_cot = gain_row * normed_cot
        mean = jnp.mean(scaled_cot * v, axis=-1, keepdims=True)
        result[1, s] = (
            cots[s].astype(f32) + inverse_rms * scaled_cot - v * (inverse_rms * inverse_rms * inverse_rms) * mean
        ).astype(bf16)
        saves += [
            pltpu.make_async_copy(result.at[0, s], block_output.at[s], out_sems.at[2 * s]),
            pltpu.make_async_copy(result.at[1, s], token_gradient.at[s], out_sems.at[2 * s + 1]),
        ]
        saves[-2].start()
        saves[-1].start()
        gain_sum += jnp.sum(normed_cot * v * inverse_rms, axis=0, keepdims=True)
    gain_rows[...] = jnp.zeros((16, 384), f32)
    for z in range(16):
        gain_rows[z : z + 1, 0:48] = gain_sum[:, 48 * z : 48 * z + 48]
    for c in saves:
        c.wait()


def split_high_low(v):
    high = v.astype(bf16).astype(f32)
    return high, v - high


def plane_kernel(given, gain_rows, out, rows):
    total = given[0].astype(f32)
    for i in range(1, 16):
        total += given[i].astype(f32)
    rows[...] = total
    for z in range(16):
        high, low = split_high_low(gain_rows[z : z + 1])
        out[z] = jnp.concatenate([rows[6 * z : 6 * z + 6], high, low]).astype(bf16)


def column_kernel(given, out):
    total = given[0].astype(f32)
    for z in range(1, 16):
        total += given[z].astype(f32)
    high, low = split_high_low(total[6:7] + total[7:8])
    block = jnp.concatenate([total[0:6], high, low]).astype(bf16)
    for i in range(32):
        out[i] = block


def final_kernel(given, perm, taps, proj, gain, rows):
    scale = 1.0 / 64
    for q in range(4):
        for k in range(3):
            for half in range(2):
                block = given[(q * 3 + k) * 2 + half].astype(f32)
                taps[k, 6 * q : 6 * q + 6, 384 * half : 384 * half + 384] = block[0:6] * scale
    for u in range(8):
        rows[6 * u : 6 * u + 6] = given[24 + u].astype(f32)[0:6]
    proj[...] = dot(rows[...].astype(bf16), perm[...], 1, 1) * scale
    total = given[0].astype(f32)
    for i in range(1, 32):
        total += given[i].astype(f32)
    gain[...] = ((total[6:7] + total[7:8])[:, 0:48] * scale).reshape(48)


def call(kernel, out, ins, outs, name, room, scratch=(), **more):
    return pl.pallas_call(
        kernel,
        out_shape=out,
        in_specs=ins,
        out_specs=outs,
        scratch_shapes=scratch,
        compiler_params=pltpu.CompilerParams(vmem_limit_bytes=room * MB),
        name=name,
        **more,
    )


def shape(dims, kind):
    return jax.ShapeDtypeStruct(dims, kind)


HALF = shape((16, 96, 384), bf16)
ROWS = shape((SEQS, BINS, CHANNELS), bf16)
LOCAL = pltpu.VMEM((SEQS, BINS, CHANNELS), bf16)
MATRIX = pltpu.VMEM((CHANNELS, CHANNELS), bf16)


def waits(count):
    return pltpu.SemaphoreType.DMA((count,))


def make_piece(part, taps, proj, perm):
    return call(
        piece_kernel, shape((16, 8, 384), bf16), [SMEM] + [VMEM] * 3, VMEM, "piece", 6, [pltpu.VMEM((32, 8, 384), f32)]
    )(part, taps, proj, perm)


def make_stack(given):
    return call(stack_kernel, HALF, [VMEM], VMEM, "stack", 6, [pltpu.VMEM((96, 384), f32)])(given)


def make_norm(tokens, gain, cot):
    edge = shape((SEQS, 3 * STEP, CHANNELS), bf16)
    return call(norm_kernel, [edge, edge], [FAR] * 3, [VMEM] * 2, "norm", 12, [LOCAL, pltpu.VMEM((CHANNELS,), f32), waits(5)])(
        tokens, gain, cot
    )


def make_ready(tokens, gain, cot, perm, up, down, before, after):
    return call(
        ready_kernel,
        [
            shape((SEQS, BINS + 4 * STEP, CHANNELS), bf16),
            shape((SEQS, EXT, CHANNELS), bf16),
            shape((SEQS, BINS, CHANNELS), f32),
        ],
        [FAR, VMEM, FAR, FAR] + [VMEM] * 4,
        [VMEM] * 3,
        "ready",
        20,
        [LOCAL, LOCAL, MATRIX, waits(3)],
    )(tokens, gain, cot, perm, up, down, before, after)


def make_main(core, mine, other, act, cot):
    return call(
        main_kernel,
        [
            HALF,
            HALF,
            shape((SEQS, EXT, HIDDEN), bf16),
            shape((SEQS, BINS, HIDDEN), bf16),
            shape((3, HIDDEN, CHANNELS), bf16),
            shape((CHANNELS, HIDDEN), bf16),
        ],
        [SMEM, HBM, HBM, VMEM, VMEM],
        [HBM] * 2 + [VMEM] * 4,
        "main",
        24,
        [pltpu.VMEM((32, 96, 384), bf16), waits(32), waits(2)],
    )(core, mine, other, act, cot)


def make_pair(a, b):
    return call(pair_kernel, HALF, [VMEM] * 2, VMEM, "pair", 8)(a, b)


def make_tail(taps, proj, sum_cot, hidden, slope, tokens, gain, cot, perm):
    return call(
        tail_kernel,
        [ROWS, ROWS, shape((16, 384), f32)],
        [VMEM] * 5 + [FAR, VMEM, FAR, FAR],
        [FAR, FAR, VMEM],
        "tail",
        24,
        [LOCAL, LOCAL, MATRIX, pltpu.VMEM((2, SEQS, BINS, CHANNELS), bf16), waits(3), waits(4)],
    )(taps, proj, sum_cot, hidden, slope, tokens, gain, cot, perm)


def make_plane(given, gain_rows):
    return call(
        plane_kernel, shape((16, 8, 384), bf16), [VMEM] * 2, VMEM, "plane", 6, [pltpu.VMEM((96, 384), f32)]
    )(given, gain_rows)


def make_column(given):
    return call(column_kernel, shape((32, 8, 384), bf16), [VMEM], VMEM, "column", 6)(given)


def make_final(given, perm):
    return call(
        final_kernel,
        [shape((3, 24, CHANNELS), f32), shape((48, 384), f32), shape((48,), f32)],
        [VMEM] * 2,
        [VMEM] * 3,
        "final",
        6,
        [pltpu.VMEM((48, 384), f32)],
    )(given, perm)


def on_device(tokens, norm_gain, dilated_weight, output_weight, cotangent):
    yx = ("y", "x")
    swap = [(0, 1), (1, 0)]
    core = lax.axis_index("c").reshape(1)
    part = core * 16 + lax.axis_index(yx)
    lane_perm = jnp.asarray(permutation(4, 16, 6), bf16)
    row_perm = jnp.asarray(permutation(8, 16, 6), bf16)

    tokens = pltpu.with_memory_space_constraint(tokens, pltpu.HBM)
    cotangent = pltpu.with_memory_space_constraint(cotangent, pltpu.HBM)
    up, down = make_norm(tokens, pltpu.with_memory_space_constraint(norm_gain, pltpu.HBM), cotangent)
    before = lax.ppermute(up, "z", [(i, i + 1) for i in range(15)])
    after = lax.ppermute(down, "z", [(i + 1, i) for i in range(15)])

    piece = make_piece(part, dilated_weight.transpose(0, 2, 1), output_weight.T, lane_perm)
    from_z = lax.all_to_all(piece, "z", 0, 0)
    from_z, before, after = lax.optimization_barrier((from_z, before, after))
    mine = lax.all_to_all(make_stack(from_z), yx, 0, 0)
    mine, before, after = lax.optimization_barrier((mine, before, after))
    other = lax.ppermute(mine, "c", swap)
    act, cot_perm, slope = make_ready(tokens, norm_gain, cotangent, row_perm, up, down, before, after)

    keep, send, sum_cot, hidden, every_tap, every_proj = make_main(core, mine, other, act, cot_perm)
    received = lax.ppermute(send, "c", swap)
    residual_output, token_cotangent, gain_rows = make_tail(
        every_tap, every_proj, sum_cot, hidden, slope, tokens, norm_gain, cotangent, row_perm
    )
    received, residual_output, token_cotangent, gain_rows = lax.optimization_barrier(
        (received, residual_output, token_cotangent, gain_rows)
    )
    plane = lax.all_to_all(make_pair(keep, received), yx, 0, 0)
    column = lax.all_to_all(make_plane(plane, gain_rows), "z", 0, 0)
    spread = lax.all_to_all(make_column(column), ("c", "y", "x"), 0, 0)
    taps, proj, gain = make_final(spread, lane_perm)
    return residual_output, token_cotangent, taps.transpose(0, 2, 1), proj.T, gain


def solution(mesh):
    fine = Mesh(mesh.devices.reshape(4, 4, 2, 16), ("y", "x", "c", "z"))
    dp = ("y", "x", "c")
    rows = P(dp, "z", None)
    in_specs = (rows, P(), P(None, None, "z"), P(None, "z"), rows)
    out_specs = (rows, rows, P(None, None, "z"), P(None, "z"), P("z"))
    return jax.shard_map(on_device, mesh=fine, in_specs=in_specs, out_specs=out_specs, check_vma=False)
```

```python
import jax
import jax.numpy as jnp
import numpy as np
from jax import lax
from jax.experimental import pallas as pl
from jax.experimental.pallas import tpu as pltpu
from jax.sharding import Mesh, PartitionSpec as P

STEP = 64
SEQS = 2
BINS = 256
CHANNELS = 768
HIDDEN = 384
EXT = BINS + 2 * STEP
gelu_scale = 0.7978845608
cubic_term = 0.044715
epsilon = 1e-06
bf16 = jnp.bfloat16
f32 = jnp.float32
SMEM = pl.BlockSpec(memory_space=pltpu.SMEM)
VMEM = pl.BlockSpec(memory_space=pltpu.VMEM)
FAR = pl.BlockSpec(memory_space=pltpu.HBM)
MB = 1024 * 1024
TILE = 32


def permutation(outer, inner, width):
    size = outer * inner * width
    order = np.arange(size).reshape(inner, outer, width).transpose(1, 0, 2).reshape(-1)
    matrix = np.zeros((size, size), np.float32)
    matrix[order, np.arange(size)] = 1.0
    return matrix


def dot(a, b, ca, cb):
    return lax.dot_general(a, b, (((ca,), (cb,)), ((), ())), preferred_element_type=f32)


def tanh_of(v):
    return jnp.tanh(gelu_scale * (v + cubic_term * v * v * v))


def activate(v, t):
    return 0.5 * v * (1.0 + t)


def derivative(v, t):
    return 0.5 * (1.0 + t) + 0.5 * v * (1.0 - t * t) * gelu_scale * (1.0 + 3.0 * cubic_term * v * v)


def inverse_rms_of(v):
    return lax.rsqrt(jnp.mean(v * v, axis=-1, keepdims=True) + epsilon)


def piece_kernel(part, taps, proj, perm, out, pieces):
    for k in range(3):
        tap = taps[k].astype(f32)
        for q in range(4):
            for half in range(2):
                pieces[(q * 3 + k) * 2 + half, 0:6] = tap[6 * q : 6 * q + 6, half * 384 : half * 384 + 384]
    rows = dot(proj[...], perm[...], 1, 0)
    for u in range(8):
        pieces[24 + u, 0:6] = rows[6 * u : 6 * u + 6]
    pieces[:, 6:8] = jnp.zeros((32, 2, 384), f32)
    own = pieces[part[0]].astype(bf16)
    for z in range(16):
        out[z] = own


def stack_kernel(given, out, rows):
    for z in range(16):
        rows[6 * z : 6 * z + 6] = given[z].astype(f32)[0:6]
    packed = rows[...].astype(bf16)
    for i in range(16):
        out[i] = packed


def run(pairs, sems):
    copies = [pltpu.make_async_copy(a, b, sems.at[i]) for i, (a, b) in enumerate(pairs)]
    for c in copies:
        c.start()
    return copies


def norm_kernel(tokens, gain_in, cot, up, down, rows, gain, sems):
    loads = [(tokens.at[s], rows.at[s]) for s in range(SEQS)]
    loads += [
        (gain_in, gain),
        (cot.at[:, BINS - STEP :], up.at[:, 2 * STEP :]),
        (cot.at[:, 0:STEP], down.at[:, 2 * STEP :]),
    ]
    loads = run(loads, sems)
    loads[SEQS].wait()
    gain_row = gain[...].reshape(1, CHANNELS)
    for s in range(SEQS):
        loads[s].wait()
        for r in range(0, BINS, TILE):
            v = rows[s, r : r + TILE].astype(f32)
            normed = v * inverse_rms_of(v) * gain_row
            edge, at = (down, r) if r < 2 * STEP else (up, r - 2 * STEP)
            edge[s, at : at + TILE] = activate(normed, tanh_of(normed)).astype(bf16)
    for c in loads[SEQS + 1 :]:
        c.wait()


def ready_kernel(
    tokens, gain, cot, perm, up, down, before, after,
    act, cot_perm, slope,
    rows, cots, sems,
):
    loads = [(cot.at[s], cots.at[s]) for s in range(SEQS)] + [(tokens.at[s], rows.at[s]) for s in range(SEQS)]
    loads = run(loads, sems)
    half = 2 * STEP
    act[:, 0:half] = before[:, 0:half]
    act[:, half : 2 * half] = down[:, 0:half]
    act[:, 2 * half : 3 * half] = up[:, 0:half]
    act[:, 3 * half :] = after[:, 0:half]
    order = perm[...]
    gain_row = gain[...].reshape(1, CHANNELS)
    for s in range(SEQS):
        edges = dot(jnp.concatenate([before[s, half:], after[s, half:]]), order, 1, 0).astype(bf16)
        cot_perm[s, 0:STEP] = edges[0:STEP]
        cot_perm[s, STEP + BINS :] = edges[STEP:]
    for s in range(SEQS):
        loads[s].wait()
        cot_perm[s, STEP : STEP + BINS] = dot(cots[s], order, 1, 0).astype(bf16)
        loads[SEQS + s].wait()
        for r in range(0, BINS, TILE):
            v = rows[s, r : r + TILE].astype(f32)
            normed = v * inverse_rms_of(v) * gain_row
            slope[s, r : r + TILE] = derivative(normed, tanh_of(normed))


def place(lower, upper, taps, proj):
    for p in range(32):
        piece = (lower if p < 16 else upper)[p % 16]
        if p < 24:
            q, k, half = p // 6, p % 6 // 2, p % 2
            taps[k, 96 * q : 96 * q + 96, 384 * half : 384 * half + 384] = piece
        else:
            proj[96 * (p - 24) : 96 * (p - 24) + 96] = piece


def main_kernel(
    core, mine, other, act, cot,
    keep, send, sum_cot, hidden, taps, proj,
    grad,
):
    own = BINS
    pl.when(core[0] == 0)(lambda: place(mine, other, taps, proj))
    pl.when(core[0] == 1)(lambda: place(other, mine, taps, proj))
    for s in range(SEQS):
        total = dot(act[s, 0:EXT], taps[0], 1, 1)
        total += dot(act[s, STEP : STEP + EXT], taps[1], 1, 1)
        total += dot(act[s, 2 * STEP : 2 * STEP + EXT], taps[2], 1, 1)
        hidden_cot = dot(cot[s], proj[...], 1, 0)
        for r in range(0, EXT, TILE):
            v = total[r : r + TILE]
            t = tanh_of(v)
            if STEP <= r < STEP + own:
                hidden[s, r - STEP : r - STEP + TILE] = activate(v, t).astype(bf16)
            rounded = hidden_cot[r : r + TILE].astype(bf16).astype(f32)
            sum_cot[s, r : r + TILE] = (rounded * derivative(v, t)).astype(bf16)
    centre = jnp.concatenate([sum_cot[s, STEP : STEP + own] for s in range(SEQS)])
    for k in range(3):
        rows = jnp.concatenate([act[s, STEP * (k + 1) : STEP * (k + 1) + own] for s in range(SEQS)])
        g = dot(centre, rows, 0, 0).astype(bf16)
        for q in range(4):
            for half in range(2):
                grad[(q * 3 + k) * 2 + half] = g[96 * q : 96 * q + 96, 384 * half : 384 * half + 384]
    rows = jnp.concatenate([cot[s, STEP : STEP + own] for s in range(SEQS)])
    g = dot(rows, jnp.concatenate([hidden[s] for s in range(SEQS)]), 0, 0).astype(bf16)
    for u in range(8):
        grad[24 + u] = g[96 * u : 96 * u + 96]

    @pl.when(core[0] == 0)
    def _():
        keep[...] = grad[0:16]
        send[...] = grad[16:32]

    @pl.when(core[0] == 1)
    def _():
        keep[...] = grad[16:32]
        send[...] = grad[0:16]


def pair_kernel(a, b, out):
    out[...] = (a[...].astype(f32) + b[...].astype(f32)).astype(bf16)


def tail_kernel(
    taps, proj, sum_cot, hidden, slope, tokens, gain, cot, perm,
    block_output, token_gradient, gain_rows,
    rows, cots, result, sems, out_sems,
):
    loads = [(tokens.at[s], rows.at[s]) for s in range(SEQS)] + [(cot.at[s], cots.at[s]) for s in range(SEQS)]
    loads = run(loads, sems)
    natural = dot(perm[...], proj[...], 1, 0).astype(bf16)
    gain_row = gain[...].reshape(1, CHANNELS)
    gain_sum = jnp.zeros((1, CHANNELS), f32)
    saves = []
    for s in range(SEQS):
        total = dot(sum_cot[s, 2 * STEP : 2 * STEP + BINS], taps[0], 1, 0)
        total += dot(sum_cot[s, STEP : STEP + BINS], taps[1], 1, 0)
        total += dot(sum_cot[s, 0:BINS], taps[2], 1, 0)
        projected = dot(hidden[s], natural, 1, 1)
        loads[s].wait()
        loads[SEQS + s].wait()
        for r in range(0, BINS, TILE):
            at = slice(r, r + TILE)
            v = rows[s, at].astype(f32)
            result[0, s, at] = (v + projected[at]).astype(bf16)
            normed_cot = total[at].astype(bf16).astype(f32) * slope[s, at]
            inverse_rms = inverse_rms_of(v)
            scaled_cot = gain_row * normed_cot
            mean = jnp.mean(scaled_cot * v, axis=-1, keepdims=True)
            result[1, s, at] = (
                cots[s, at].astype(f32) + inverse_rms * scaled_cot - v * (inverse_rms * inverse_rms * inverse_rms) * mean
            ).astype(bf16)
            gain_sum += jnp.sum(normed_cot * v * inverse_rms, axis=0, keepdims=True)
        saves += [
            pltpu.make_async_copy(result.at[0, s], block_output.at[s], out_sems.at[2 * s]),
            pltpu.make_async_copy(result.at[1, s], token_gradient.at[s], out_sems.at[2 * s + 1]),
        ]
        saves[-2].start()
        saves[-1].start()
    gain_rows[...] = jnp.zeros((16, 384), f32)
    for z in range(16):
        gain_rows[z : z + 1, 0:48] = gain_sum[:, 48 * z : 48 * z + 48]
    for c in saves:
        c.wait()


def split_high_low(v):
    high = v.astype(bf16).astype(f32)
    return high, v - high


def plane_kernel(given, gain_rows, out, rows):
    total = given[0].astype(f32)
    for i in range(1, 16):
        total += given[i].astype(f32)
    rows[...] = total
    for z in range(16):
        high, low = split_high_low(gain_rows[z : z + 1])
        out[z] = jnp.concatenate([rows[6 * z : 6 * z + 6], high, low]).astype(bf16)


def column_kernel(given, out):
    total = given[0].astype(f32)
    for z in range(1, 16):
        total += given[z].astype(f32)
    high, low = split_high_low(total[6:7] + total[7:8])
    block = jnp.concatenate([total[0:6], high, low]).astype(bf16)
    for i in range(32):
        out[i] = block


def final_kernel(given, perm, taps, proj, gain, rows):
    scale = 1.0 / 64
    for q in range(4):
        for k in range(3):
            for half in range(2):
                block = given[(q * 3 + k) * 2 + half].astype(f32)
                taps[k, 6 * q : 6 * q + 6, 384 * half : 384 * half + 384] = block[0:6] * scale
    for u in range(8):
        rows[6 * u : 6 * u + 6] = given[24 + u].astype(f32)[0:6]
    proj[...] = dot(rows[...].astype(bf16), perm[...], 1, 1) * scale
    total = given[0].astype(f32)
    for i in range(1, 32):
        total += given[i].astype(f32)
    gain[...] = ((total[6:7] + total[7:8])[:, 0:48] * scale).reshape(48)


def call(kernel, out, ins, outs, name, room, scratch=(), **more):
    return pl.pallas_call(
        kernel,
        out_shape=out,
        in_specs=ins,
        out_specs=outs,
        scratch_shapes=scratch,
        compiler_params=pltpu.CompilerParams(vmem_limit_bytes=room * MB),
        name=name,
        **more,
    )


def shape(dims, kind):
    return jax.ShapeDtypeStruct(dims, kind)


HALF = shape((16, 96, 384), bf16)
ROWS = shape((SEQS, BINS, CHANNELS), bf16)
LOCAL = pltpu.VMEM((SEQS, BINS, CHANNELS), bf16)


def waits(count):
    return pltpu.SemaphoreType.DMA((count,))


def make_piece(part, taps, proj, perm):
    return call(
        piece_kernel, shape((16, 8, 384), bf16), [SMEM] + [VMEM] * 3, VMEM, "piece", 6, [pltpu.VMEM((32, 8, 384), f32)]
    )(part, taps, proj, perm)


def make_stack(given):
    return call(stack_kernel, HALF, [VMEM], VMEM, "stack", 6, [pltpu.VMEM((96, 384), f32)])(given)


def make_norm(tokens, gain, cot):
    edge = shape((SEQS, 3 * STEP, CHANNELS), bf16)
    return call(norm_kernel, [edge, edge], [FAR] * 3, [VMEM] * 2, "norm", 6, [LOCAL, pltpu.VMEM((CHANNELS,), f32), waits(5)])(
        tokens, gain, cot
    )


def make_ready(tokens, gain, cot, perm, up, down, before, after):
    return call(
        ready_kernel,
        [
            shape((SEQS, BINS + 4 * STEP, CHANNELS), bf16),
            shape((SEQS, EXT, CHANNELS), bf16),
            shape((SEQS, BINS, CHANNELS), f32),
        ],
        [FAR, VMEM, FAR] + [VMEM] * 5,
        [VMEM] * 3,
        "ready",
        10,
        [LOCAL, LOCAL, waits(4)],
    )(tokens, gain, cot, perm, up, down, before, after)


def make_main(core, mine, other, act, cot):
    return call(
        main_kernel,
        [
            HALF,
            HALF,
            shape((SEQS, EXT, HIDDEN), bf16),
            shape((SEQS, BINS, HIDDEN), bf16),
            shape((3, HIDDEN, CHANNELS), bf16),
            shape((CHANNELS, HIDDEN), bf16),
        ],
        [SMEM] + [VMEM] * 4,
        [VMEM] * 6,
        "main",
        10,
        [pltpu.VMEM((32, 96, 384), bf16)],
    )(core, mine, other, act, cot)


def make_pair(a, b):
    return call(pair_kernel, HALF, [VMEM] * 2, VMEM, "pair", 8)(a, b)


def make_tail(taps, proj, sum_cot, hidden, slope, tokens, gain, cot, perm):
    return call(
        tail_kernel,
        [ROWS, ROWS, shape((16, 384), f32)],
        [VMEM] * 5 + [FAR, VMEM, FAR, VMEM],
        [FAR, FAR, VMEM],
        "tail",
        12,
        [LOCAL, LOCAL, pltpu.VMEM((2, SEQS, BINS, CHANNELS), bf16), waits(4), waits(4)],
    )(taps, proj, sum_cot, hidden, slope, tokens, gain, cot, perm)


def make_plane(given, gain_rows):
    return call(
        plane_kernel, shape((16, 8, 384), bf16), [VMEM] * 2, VMEM, "plane", 6, [pltpu.VMEM((96, 384), f32)]
    )(given, gain_rows)


def make_column(given):
    return call(column_kernel, shape((32, 8, 384), bf16), [VMEM], VMEM, "column", 6)(given)


def make_final(given, perm):
    return call(
        final_kernel,
        [shape((3, 24, CHANNELS), f32), shape((48, 384), f32), shape((48,), f32)],
        [VMEM] * 2,
        [VMEM] * 3,
        "final",
        6,
        [pltpu.VMEM((48, 384), f32)],
    )(given, perm)


def on_device(tokens, norm_gain, dilated_weight, output_weight, cotangent):
    yx = ("y", "x")
    swap = [(0, 1), (1, 0)]
    core = lax.axis_index("c").reshape(1)
    part = core * 16 + lax.axis_index(yx)
    lane_perm = jnp.asarray(permutation(4, 16, 6), bf16)
    row_perm = jnp.asarray(permutation(8, 16, 6), bf16)

    tokens = pltpu.with_memory_space_constraint(tokens, pltpu.HBM)
    cotangent = pltpu.with_memory_space_constraint(cotangent, pltpu.HBM)
    up, down = make_norm(tokens, pltpu.with_memory_space_constraint(norm_gain, pltpu.HBM), cotangent)
    before = lax.ppermute(up, "z", [(i, i + 1) for i in range(15)])
    after = lax.ppermute(down, "z", [(i + 1, i) for i in range(15)])

    piece = make_piece(part, dilated_weight.transpose(0, 2, 1), output_weight.T, lane_perm)
    from_z = lax.all_to_all(piece, "z", 0, 0)
    from_z, before, after = lax.optimization_barrier((from_z, before, after))
    mine = lax.all_to_all(make_stack(from_z), yx, 0, 0)
    mine, before, after = lax.optimization_barrier((mine, before, after))
    other = lax.ppermute(mine, "c", swap)
    act, cot_perm, slope = make_ready(tokens, norm_gain, cotangent, row_perm, up, down, before, after)

    keep, send, sum_cot, hidden, every_tap, every_proj = make_main(core, mine, other, act, cot_perm)
    received = lax.ppermute(send, "c", swap)
    residual_output, token_cotangent, gain_rows = make_tail(
        every_tap, every_proj, sum_cot, hidden, slope, tokens, norm_gain, cotangent, row_perm
    )
    received, residual_output, token_cotangent, gain_rows = lax.optimization_barrier(
        (received, residual_output, token_cotangent, gain_rows)
    )
    plane = lax.all_to_all(make_pair(keep, received), yx, 0, 0)
    column = lax.all_to_all(make_plane(plane, gain_rows), "z", 0, 0)
    spread = lax.all_to_all(make_column(column), ("c", "y", "x"), 0, 0)
    taps, proj, gain = make_final(spread, lane_perm)
    return residual_output, token_cotangent, taps.transpose(0, 2, 1), proj.T, gain


def solution(mesh):
    fine = Mesh(mesh.devices.reshape(4, 4, 2, 16), ("y", "x", "c", "z"))
    dp = ("y", "x", "c")
    rows = P(dp, "z", None)
    in_specs = (rows, P(), P(None, None, "z"), P(None, "z"), rows)
    out_specs = (rows, rows, P(None, None, "z"), P(None, "z"), P("z"))
    return jax.shard_map(on_device, mesh=fine, in_specs=in_specs, out_specs=out_specs, check_vma=False)
```

```python
import jax
import jax.numpy as jnp
import numpy as np
from jax import lax
from jax.experimental import pallas as pl
from jax.experimental.pallas import tpu as pltpu
from jax.sharding import Mesh, PartitionSpec as P

STEP = 64
SEQS = 2
BINS = 256
CHANNELS = 768
HIDDEN = 384
EXT = BINS + 2 * STEP
gelu_scale = 0.7978845608
cubic_term = 0.044715
epsilon = 1e-06
bf16 = jnp.bfloat16
f32 = jnp.float32
SMEM = pl.BlockSpec(memory_space=pltpu.SMEM)
VMEM = pl.BlockSpec(memory_space=pltpu.VMEM)
FAR = pl.BlockSpec(memory_space=pltpu.HBM)
MB = 1024 * 1024
TILE = 32


def permutation(outer, inner, width):
    size = outer * inner * width
    order = np.arange(size).reshape(inner, outer, width).transpose(1, 0, 2).reshape(-1)
    matrix = np.zeros((size, size), np.float32)
    matrix[order, np.arange(size)] = 1.0
    return matrix


def dot(a, b, ca, cb):
    return lax.dot_general(a, b, (((ca,), (cb,)), ((), ())), preferred_element_type=f32)


def tanh_of(v):
    return jnp.tanh(gelu_scale * (v + cubic_term * v * v * v))


def activate(v, t):
    return 0.5 * v * (1.0 + t)


def derivative(v, t):
    return 0.5 * (1.0 + t) + 0.5 * v * (1.0 - t * t) * gelu_scale * (1.0 + 3.0 * cubic_term * v * v)


def inverse_rms_of(v):
    return lax.rsqrt(jnp.mean(v * v, axis=-1, keepdims=True) + epsilon)


def piece_kernel(part, taps, proj, perm, out, pieces):
    for k in range(3):
        tap = taps[k].astype(f32)
        for q in range(4):
            for half in range(2):
                pieces[(q * 3 + k) * 2 + half, 0:6] = tap[6 * q : 6 * q + 6, half * 384 : half * 384 + 384]
    rows = dot(proj[...], perm[...], 1, 0)
    for u in range(8):
        pieces[24 + u, 0:6] = rows[6 * u : 6 * u + 6]
    pieces[:, 6:8] = jnp.zeros((32, 2, 384), f32)
    own = pieces[part[0]].astype(bf16)
    for z in range(16):
        out[z] = own


def stack_kernel(given, out, rows):
    for z in range(16):
        rows[6 * z : 6 * z + 6] = given[z].astype(f32)[0:6]
    packed = rows[...].astype(bf16)
    for i in range(16):
        out[i] = packed


def run(pairs, sems):
    copies = [pltpu.make_async_copy(a, b, sems.at[i]) for i, (a, b) in enumerate(pairs)]
    for c in copies:
        c.start()
    return copies


def norm_kernel(tokens, gain_in, cot, up, down, rows, gain, sems):
    loads = [(tokens.at[s], rows.at[s]) for s in range(SEQS)]
    loads += [
        (gain_in, gain),
        (cot.at[:, BINS - STEP :], up.at[:, 2 * STEP :]),
        (cot.at[:, 0:STEP], down.at[:, 2 * STEP :]),
    ]
    loads = run(loads, sems)
    loads[SEQS].wait()
    gain_row = gain[...].reshape(1, CHANNELS)
    for s in range(SEQS):
        loads[s].wait()
        for r in range(0, BINS, TILE):
            v = rows[s, r : r + TILE].astype(f32)
            normed = v * inverse_rms_of(v) * gain_row
            edge, at = (down, r) if r < 2 * STEP else (up, r - 2 * STEP)
            edge[s, at : at + TILE] = activate(normed, tanh_of(normed)).astype(bf16)
    for c in loads[SEQS + 1 :]:
        c.wait()


def own_kernel(tokens, gain, cot, perm, cot_perm, slope, rows, cots, sems):
    loads = [(cot.at[s], cots.at[s]) for s in range(SEQS)] + [(tokens.at[s], rows.at[s]) for s in range(SEQS)]
    loads = run(loads, sems)
    order = perm[...]
    gain_row = gain[...].reshape(1, CHANNELS)
    for s in range(SEQS):
        loads[s].wait()
        cot_perm[s] = dot(cots[s], order, 1, 0).astype(bf16)
        loads[SEQS + s].wait()
        for r in range(0, BINS, TILE):
            v = rows[s, r : r + TILE].astype(f32)
            normed = v * inverse_rms_of(v) * gain_row
            slope[s, r : r + TILE] = derivative(normed, tanh_of(normed))


def ready_kernel(own, perm, up, down, before, after, act, cot_perm):
    half = 2 * STEP
    act[:, 0:half] = before[:, 0:half]
    act[:, half : 2 * half] = down[:, 0:half]
    act[:, 2 * half : 3 * half] = up[:, 0:half]
    act[:, 3 * half :] = after[:, 0:half]
    edges = [t[s, half:] for s in range(SEQS) for t in (before, after)]
    edges = dot(jnp.concatenate(edges), perm[...], 1, 0).astype(bf16)
    for s in range(SEQS):
        at = 2 * s * STEP
        cot_perm[s, 0:STEP] = edges[at : at + STEP]
        cot_perm[s, STEP : STEP + BINS] = own[s]
        cot_perm[s, STEP + BINS :] = edges[at + STEP : at + 2 * STEP]


def place(lower, upper, taps, proj):
    for p in range(32):
        piece = (lower if p < 16 else upper)[p % 16]
        if p < 24:
            q, k, half = p // 6, p % 6 // 2, p % 2
            taps[k, 96 * q : 96 * q + 96, 384 * half : 384 * half + 384] = piece
        else:
            proj[96 * (p - 24) : 96 * (p - 24) + 96] = piece


def main_kernel(
    core, mine, other, act, cot,
    keep, send, sum_cot, hidden, taps, proj,
    grad,
):
    own = BINS
    pl.when(core[0] == 0)(lambda: place(mine, other, taps, proj))
    pl.when(core[0] == 1)(lambda: place(other, mine, taps, proj))
    for s in range(SEQS):
        total = dot(act[s, 0:EXT], taps[0], 1, 1)
        total += dot(act[s, STEP : STEP + EXT], taps[1], 1, 1)
        total += dot(act[s, 2 * STEP : 2 * STEP + EXT], taps[2], 1, 1)
        hidden_cot = dot(cot[s], proj[...], 1, 0)
        for r in range(0, EXT, TILE):
            v = total[r : r + TILE]
            t = tanh_of(v)
            if STEP <= r < STEP + own:
                hidden[s, r - STEP : r - STEP + TILE] = activate(v, t).astype(bf16)
            rounded = hidden_cot[r : r + TILE].astype(bf16).astype(f32)
            sum_cot[s, r : r + TILE] = (rounded * derivative(v, t)).astype(bf16)
    centre = jnp.concatenate([sum_cot[s, STEP : STEP + own] for s in range(SEQS)])
    for k in range(3):
        rows = jnp.concatenate([act[s, STEP * (k + 1) : STEP * (k + 1) + own] for s in range(SEQS)])
        g = dot(centre, rows, 0, 0).astype(bf16)
        for q in range(4):
            for half in range(2):
                grad[(q * 3 + k) * 2 + half] = g[96 * q : 96 * q + 96, 384 * half : 384 * half + 384]
    rows = jnp.concatenate([cot[s, STEP : STEP + own] for s in range(SEQS)])
    g = dot(rows, jnp.concatenate([hidden[s] for s in range(SEQS)]), 0, 0).astype(bf16)
    for u in range(8):
        grad[24 + u] = g[96 * u : 96 * u + 96]

    @pl.when(core[0] == 0)
    def _():
        keep[...] = grad[0:16]
        send[...] = grad[16:32]

    @pl.when(core[0] == 1)
    def _():
        keep[...] = grad[16:32]
        send[...] = grad[0:16]


def pair_kernel(a, b, out):
    out[...] = (a[...].astype(f32) + b[...].astype(f32)).astype(bf16)


def tail_kernel(
    taps, proj, sum_cot, hidden, slope, tokens, gain, cot, perm,
    block_output, token_gradient, gain_rows,
    rows, cots, result, sems, out_sems,
):
    loads = [(tokens.at[s], rows.at[s]) for s in range(SEQS)] + [(cot.at[s], cots.at[s]) for s in range(SEQS)]
    loads = run(loads, sems)
    natural = dot(perm[...], proj[...], 1, 0).astype(bf16)
    gain_row = gain[...].reshape(1, CHANNELS)
    gain_sum = jnp.zeros((1, CHANNELS), f32)
    saves = []
    for s in range(SEQS):
        total = dot(sum_cot[s, 2 * STEP : 2 * STEP + BINS], taps[0], 1, 0)
        total += dot(sum_cot[s, STEP : STEP + BINS], taps[1], 1, 0)
        total += dot(sum_cot[s, 0:BINS], taps[2], 1, 0)
        projected = dot(hidden[s], natural, 1, 1)
        loads[s].wait()
        loads[SEQS + s].wait()
        for r in range(0, BINS, TILE):
            at = slice(r, r + TILE)
            v = rows[s, at].astype(f32)
            result[0, s, at] = (v + projected[at]).astype(bf16)
            normed_cot = total[at].astype(bf16).astype(f32) * slope[s, at]
            inverse_rms = inverse_rms_of(v)
            scaled_cot = gain_row * normed_cot
            mean = jnp.mean(scaled_cot * v, axis=-1, keepdims=True)
            result[1, s, at] = (
                cots[s, at].astype(f32) + inverse_rms * scaled_cot - v * (inverse_rms * inverse_rms * inverse_rms) * mean
            ).astype(bf16)
            gain_sum += jnp.sum(normed_cot * v * inverse_rms, axis=0, keepdims=True)
        saves += [
            pltpu.make_async_copy(result.at[0, s], block_output.at[s], out_sems.at[2 * s]),
            pltpu.make_async_copy(result.at[1, s], token_gradient.at[s], out_sems.at[2 * s + 1]),
        ]
        saves[-2].start()
        saves[-1].start()
    gain_rows[...] = jnp.zeros((16, 384), f32)
    for z in range(16):
        gain_rows[z : z + 1, 0:48] = gain_sum[:, 48 * z : 48 * z + 48]
    for c in saves:
        c.wait()


def split_high_low(v):
    high = v.astype(bf16).astype(f32)
    return high, v - high


def plane_kernel(given, gain_rows, out, rows):
    total = given[0].astype(f32)
    for i in range(1, 16):
        total += given[i].astype(f32)
    rows[...] = total
    for z in range(16):
        high, low = split_high_low(gain_rows[z : z + 1])
        out[z] = jnp.concatenate([rows[6 * z : 6 * z + 6], high, low]).astype(bf16)


def column_kernel(given, out):
    total = given[0].astype(f32)
    for z in range(1, 16):
        total += given[z].astype(f32)
    high, low = split_high_low(total[6:7] + total[7:8])
    block = jnp.concatenate([total[0:6], high, low]).astype(bf16)
    for i in range(32):
        out[i] = block


def final_kernel(given, perm, taps, proj, gain, rows):
    scale = 1.0 / 64
    for q in range(4):
        for k in range(3):
            for half in range(2):
                block = given[(q * 3 + k) * 2 + half].astype(f32)
                taps[k, 6 * q : 6 * q + 6, 384 * half : 384 * half + 384] = block[0:6] * scale
    for u in range(8):
        rows[6 * u : 6 * u + 6] = given[24 + u].astype(f32)[0:6]
    proj[...] = dot(rows[...].astype(bf16), perm[...], 1, 1) * scale
    total = given[0].astype(f32)
    for i in range(1, 32):
        total += given[i].astype(f32)
    gain[...] = ((total[6:7] + total[7:8])[:, 0:48] * scale).reshape(48)


def call(kernel, out, ins, outs, name, room, scratch=(), **more):
    return pl.pallas_call(
        kernel,
        out_shape=out,
        in_specs=ins,
        out_specs=outs,
        scratch_shapes=scratch,
        compiler_params=pltpu.CompilerParams(vmem_limit_bytes=room * MB),
        name=name,
        **more,
    )


def shape(dims, kind):
    return jax.ShapeDtypeStruct(dims, kind)


HALF = shape((16, 96, 384), bf16)
ROWS = shape((SEQS, BINS, CHANNELS), bf16)
LOCAL = pltpu.VMEM((SEQS, BINS, CHANNELS), bf16)


def waits(count):
    return pltpu.SemaphoreType.DMA((count,))


def make_piece(part, taps, proj, perm):
    return call(
        piece_kernel, shape((16, 8, 384), bf16), [SMEM] + [VMEM] * 3, VMEM, "piece", 6, [pltpu.VMEM((32, 8, 384), f32)]
    )(part, taps, proj, perm)


def make_stack(given):
    return call(stack_kernel, HALF, [VMEM], VMEM, "stack", 6, [pltpu.VMEM((96, 384), f32)])(given)


def make_norm(tokens, gain, cot):
    edge = shape((SEQS, 3 * STEP, CHANNELS), bf16)
    return call(norm_kernel, [edge, edge], [FAR] * 3, [VMEM] * 2, "norm", 6, [LOCAL, pltpu.VMEM((CHANNELS,), f32), waits(5)])(
        tokens, gain, cot
    )


def make_own(tokens, gain, cot, perm):
    return call(
        own_kernel,
        [ROWS, shape((SEQS, BINS, CHANNELS), f32)],
        [FAR, VMEM, FAR, VMEM],
        [VMEM] * 2,
        "own",
        10,
        [LOCAL, LOCAL, waits(4)],
    )(tokens, gain, cot, perm)


def make_ready(own, perm, up, down, before, after):
    return call(
        ready_kernel,
        [
            shape((SEQS, BINS + 4 * STEP, CHANNELS), bf16),
            shape((SEQS, EXT, CHANNELS), bf16),
        ],
        [VMEM] * 6,
        [VMEM] * 2,
        "ready",
        8,
    )(own, perm, up, down, before, after)


def make_main(core, mine, other, act, cot):
    return call(
        main_kernel,
        [
            HALF,
            HALF,
            shape((SEQS, EXT, HIDDEN), bf16),
            shape((SEQS, BINS, HIDDEN), bf16),
            shape((3, HIDDEN, CHANNELS), bf16),
            shape((CHANNELS, HIDDEN), bf16),
        ],
        [SMEM] + [VMEM] * 4,
        [VMEM] * 6,
        "main",
        10,
        [pltpu.VMEM((32, 96, 384), bf16)],
    )(core, mine, other, act, cot)


def make_pair(a, b):
    return call(pair_kernel, HALF, [VMEM] * 2, VMEM, "pair", 8)(a, b)


def make_tail(taps, proj, sum_cot, hidden, slope, tokens, gain, cot, perm):
    return call(
        tail_kernel,
        [ROWS, ROWS, shape((16, 384), f32)],
        [VMEM] * 5 + [FAR, VMEM, FAR, VMEM],
        [FAR, FAR, VMEM],
        "tail",
        12,
        [LOCAL, LOCAL, pltpu.VMEM((2, SEQS, BINS, CHANNELS), bf16), waits(4), waits(4)],
    )(taps, proj, sum_cot, hidden, slope, tokens, gain, cot, perm)


def make_plane(given, gain_rows):
    return call(
        plane_kernel, shape((16, 8, 384), bf16), [VMEM] * 2, VMEM, "plane", 6, [pltpu.VMEM((96, 384), f32)]
    )(given, gain_rows)


def make_column(given):
    return call(column_kernel, shape((32, 8, 384), bf16), [VMEM], VMEM, "column", 6)(given)


def make_final(given, perm):
    return call(
        final_kernel,
        [shape((3, 24, CHANNELS), f32), shape((48, 384), f32), shape((48,), f32)],
        [VMEM] * 2,
        [VMEM] * 3,
        "final",
        6,
        [pltpu.VMEM((48, 384), f32)],
    )(given, perm)


def on_device(tokens, norm_gain, dilated_weight, output_weight, cotangent):
    yx = ("y", "x")
    swap = [(0, 1), (1, 0)]
    core = lax.axis_index("c").reshape(1)
    part = core * 16 + lax.axis_index(yx)
    lane_perm = jnp.asarray(permutation(4, 16, 6), bf16)
    row_perm = jnp.asarray(permutation(8, 16, 6), bf16)

    tokens = pltpu.with_memory_space_constraint(tokens, pltpu.HBM)
    cotangent = pltpu.with_memory_space_constraint(cotangent, pltpu.HBM)
    piece = make_piece(part, dilated_weight.transpose(0, 2, 1), output_weight.T, lane_perm)
    up, down = make_norm(tokens, pltpu.with_memory_space_constraint(norm_gain, pltpu.HBM), cotangent)
    from_z = lax.all_to_all(piece, "z", 0, 0)
    before = lax.ppermute(up, "z", [(i, i + 1) for i in range(15)])
    after = lax.ppermute(down, "z", [(i + 1, i) for i in range(15)])
    own, slope = make_own(tokens, norm_gain, cotangent, row_perm)
    from_z, before, after, own, slope = lax.optimization_barrier((from_z, before, after, own, slope))
    mine = lax.all_to_all(make_stack(from_z), yx, 0, 0)
    mine, before, after = lax.optimization_barrier((mine, before, after))
    other = lax.ppermute(mine, "c", swap)
    act, cot_perm = make_ready(own, row_perm, up, down, before, after)

    keep, send, sum_cot, hidden, every_tap, every_proj = make_main(core, mine, other, act, cot_perm)
    received = lax.ppermute(send, "c", swap)
    residual_output, token_cotangent, gain_rows = make_tail(
        every_tap, every_proj, sum_cot, hidden, slope, tokens, norm_gain, cotangent, row_perm
    )
    received, residual_output, token_cotangent, gain_rows = lax.optimization_barrier(
        (received, residual_output, token_cotangent, gain_rows)
    )
    plane = lax.all_to_all(make_pair(keep, received), yx, 0, 0)
    column = lax.all_to_all(make_plane(plane, gain_rows), "z", 0, 0)
    spread = lax.all_to_all(make_column(column), ("c", "y", "x"), 0, 0)
    taps, proj, gain = make_final(spread, lane_perm)
    return residual_output, token_cotangent, taps.transpose(0, 2, 1), proj.T, gain


def solution(mesh):
    fine = Mesh(mesh.devices.reshape(4, 4, 2, 16), ("y", "x", "c", "z"))
    dp = ("y", "x", "c")
    rows = P(dp, "z", None)
    in_specs = (rows, P(), P(None, None, "z"), P(None, "z"), rows)
    out_specs = (rows, rows, P(None, None, "z"), P(None, "z"), P("z"))
    return jax.shard_map(on_device, mesh=fine, in_specs=in_specs, out_specs=out_specs, check_vma=False)
```

```python
import jax
import jax.numpy as jnp
import numpy as np
from jax import lax
from jax.experimental import pallas as pl
from jax.experimental.pallas import tpu as pltpu
from jax.sharding import Mesh, PartitionSpec as P

STEP = 64
SEQS = 2
BINS = 256
CHANNELS = 768
HIDDEN = 384
EXT = BINS + 2 * STEP
gelu_scale = 0.7978845608
cubic_term = 0.044715
epsilon = 1e-06
bf16 = jnp.bfloat16
f32 = jnp.float32
SMEM = pl.BlockSpec(memory_space=pltpu.SMEM)
VMEM = pl.BlockSpec(memory_space=pltpu.VMEM)
FAR = pl.BlockSpec(memory_space=pltpu.HBM)
MB = 1024 * 1024
TILE = 32


def permutation(outer, inner, width):
    size = outer * inner * width
    order = np.arange(size).reshape(inner, outer, width).transpose(1, 0, 2).reshape(-1)
    matrix = np.zeros((size, size), np.float32)
    matrix[order, np.arange(size)] = 1.0
    return matrix


def dot(a, b, ca, cb):
    return lax.dot_general(a, b, (((ca,), (cb,)), ((), ())), preferred_element_type=f32)


def tanh_of(v):
    return jnp.tanh(gelu_scale * (v + cubic_term * v * v * v))


def activate(v, t):
    return 0.5 * v * (1.0 + t)


def derivative(v, t):
    return 0.5 * (1.0 + t) + 0.5 * v * (1.0 - t * t) * gelu_scale * (1.0 + 3.0 * cubic_term * v * v)


def inverse_rms_of(v):
    return lax.rsqrt(jnp.mean(v * v, axis=-1, keepdims=True) + epsilon)


def piece_kernel(part, taps, proj, perm, out, pieces):
    for k in range(3):
        tap = taps[k].astype(f32)
        for q in range(4):
            for half in range(2):
                pieces[(q * 3 + k) * 2 + half, 0:6] = tap[6 * q : 6 * q + 6, half * 384 : half * 384 + 384]
    rows = dot(proj[...], perm[...], 1, 0)
    for u in range(8):
        pieces[24 + u, 0:6] = rows[6 * u : 6 * u + 6]
    pieces[:, 6:8] = jnp.zeros((32, 2, 384), f32)
    own = pieces[part[0]].astype(bf16)
    for z in range(16):
        out[z] = own


def stack_kernel(given, out, rows):
    for z in range(16):
        rows[6 * z : 6 * z + 6] = given[z].astype(f32)[0:6]
    packed = rows[...].astype(bf16)
    for i in range(16):
        out[i] = packed


def run(pairs, sems):
    copies = [pltpu.make_async_copy(a, b, sems.at[i]) for i, (a, b) in enumerate(pairs)]
    for c in copies:
        c.start()
    return copies


def norm_kernel(tokens, gain_in, cot, up, down, rows, gain, sems):
    parts = [(s, pl.ds(r, BINS // 2)) for s in range(SEQS) for r in (0, BINS // 2)]
    loads = [(gain_in, gain)] + [(tokens.at[s, at], rows.at[s, at]) for s, at in parts]
    loads += [
        (cot.at[:, BINS - STEP :], up.at[:, 2 * STEP :]),
        (cot.at[:, 0:STEP], down.at[:, 2 * STEP :]),
    ]
    loads = run(loads, sems)
    loads[0].wait()
    gain_row = gain[...].reshape(1, CHANNELS)
    for s in range(SEQS):
        for r in range(0, BINS, TILE):
            if r % (BINS // 2) == 0:
                loads[1 + 2 * s + r // (BINS // 2)].wait()
            v = rows[s, r : r + TILE].astype(f32)
            normed = v * inverse_rms_of(v) * gain_row
            edge, at = (down, r) if r < 2 * STEP else (up, r - 2 * STEP)
            edge[s, at : at + TILE] = activate(normed, tanh_of(normed)).astype(bf16)
    for c in loads[1 + 2 * SEQS :]:
        c.wait()


def ready_kernel(
    rows, gain, cots, perm, up, down, before, after,
    act, cot_perm, slope,
):
    half = 2 * STEP
    act[:, 0:half] = before[:, 0:half]
    act[:, half : 2 * half] = down[:, 0:half]
    act[:, 2 * half : 3 * half] = up[:, 0:half]
    act[:, 3 * half :] = after[:, 0:half]
    order = perm[...]
    gain_row = gain[...].reshape(1, CHANNELS)
    for s in range(SEQS):
        edges = dot(jnp.concatenate([before[s, half:], after[s, half:]]), order, 1, 0).astype(bf16)
        cot_perm[s, 0:STEP] = edges[0:STEP]
        cot_perm[s, STEP + BINS :] = edges[STEP:]
    for s in range(SEQS):
        cot_perm[s, STEP : STEP + BINS] = dot(cots[s], order, 1, 0).astype(bf16)
        for r in range(0, BINS, TILE):
            v = rows[s, r : r + TILE].astype(f32)
            normed = v * inverse_rms_of(v) * gain_row
            slope[s, r : r + TILE] = derivative(normed, tanh_of(normed))


def place(lower, upper, taps, proj):
    for p in range(32):
        piece = (lower if p < 16 else upper)[p % 16]
        if p < 24:
            q, k, half = p // 6, p % 6 // 2, p % 2
            taps[k, 96 * q : 96 * q + 96, 384 * half : 384 * half + 384] = piece
        else:
            proj[96 * (p - 24) : 96 * (p - 24) + 96] = piece


def main_kernel(
    core, mine, other, act, cot,
    keep, send, sum_cot, hidden, taps, proj,
    grad,
):
    own = BINS
    pl.when(core[0] == 0)(lambda: place(mine, other, taps, proj))
    pl.when(core[0] == 1)(lambda: place(other, mine, taps, proj))
    for s in range(SEQS):
        total = dot(act[s, 0:EXT], taps[0], 1, 1)
        total += dot(act[s, STEP : STEP + EXT], taps[1], 1, 1)
        total += dot(act[s, 2 * STEP : 2 * STEP + EXT], taps[2], 1, 1)
        hidden_cot = dot(cot[s], proj[...], 1, 0)
        for r in range(0, EXT, TILE):
            v = total[r : r + TILE]
            t = tanh_of(v)
            if STEP <= r < STEP + own:
                hidden[s, r - STEP : r - STEP + TILE] = activate(v, t).astype(bf16)
            rounded = hidden_cot[r : r + TILE].astype(bf16).astype(f32)
            sum_cot[s, r : r + TILE] = (rounded * derivative(v, t)).astype(bf16)
    centre = jnp.concatenate([sum_cot[s, STEP : STEP + own] for s in range(SEQS)])
    for k in range(3):
        rows = jnp.concatenate([act[s, STEP * (k + 1) : STEP * (k + 1) + own] for s in range(SEQS)])
        g = dot(centre, rows, 0, 0).astype(bf16)
        for q in range(4):
            for half in range(2):
                grad[(q * 3 + k) * 2 + half] = g[96 * q : 96 * q + 96, 384 * half : 384 * half + 384]
    rows = jnp.concatenate([cot[s, STEP : STEP + own] for s in range(SEQS)])
    g = dot(rows, jnp.concatenate([hidden[s] for s in range(SEQS)]), 0, 0).astype(bf16)
    for u in range(8):
        grad[24 + u] = g[96 * u : 96 * u + 96]

    @pl.when(core[0] == 0)
    def _():
        keep[...] = grad[0:16]
        send[...] = grad[16:32]

    @pl.when(core[0] == 1)
    def _():
        keep[...] = grad[16:32]
        send[...] = grad[0:16]


def pair_kernel(a, b, out):
    out[...] = (a[...].astype(f32) + b[...].astype(f32)).astype(bf16)


def tail_kernel(
    taps, proj, sum_cot, hidden, slope, rows, gain, cots, perm,
    block_output, token_gradient, gain_rows,
    result, out_sems,
):
    natural = dot(perm[...], proj[...], 1, 0).astype(bf16)
    gain_row = gain[...].reshape(1, CHANNELS)
    gain_sum = jnp.zeros((1, CHANNELS), f32)
    saves = []
    for s in range(SEQS):
        total = dot(sum_cot[s, 2 * STEP : 2 * STEP + BINS], taps[0], 1, 0)
        total += dot(sum_cot[s, STEP : STEP + BINS], taps[1], 1, 0)
        total += dot(sum_cot[s, 0:BINS], taps[2], 1, 0)
        projected = dot(hidden[s], natural, 1, 1)
        for r in range(0, BINS, TILE):
            at = slice(r, r + TILE)
            v = rows[s, at].astype(f32)
            result[0, s, at] = (v + projected[at]).astype(bf16)
            normed_cot = total[at].astype(bf16).astype(f32) * slope[s, at]
            inverse_rms = inverse_rms_of(v)
            scaled_cot = gain_row * normed_cot
            mean = jnp.mean(scaled_cot * v, axis=-1, keepdims=True)
            result[1, s, at] = (
                cots[s, at].astype(f32) + inverse_rms * scaled_cot - v * (inverse_rms * inverse_rms * inverse_rms) * mean
            ).astype(bf16)
            gain_sum += jnp.sum(normed_cot * v * inverse_rms, axis=0, keepdims=True)
        saves += [
            pltpu.make_async_copy(result.at[0, s], block_output.at[s], out_sems.at[2 * s]),
            pltpu.make_async_copy(result.at[1, s], token_gradient.at[s], out_sems.at[2 * s + 1]),
        ]
        saves[-2].start()
        saves[-1].start()
    gain_rows[...] = jnp.zeros((16, 384), f32)
    for z in range(16):
        gain_rows[z : z + 1, 0:48] = gain_sum[:, 48 * z : 48 * z + 48]
    for c in saves:
        c.wait()


def split_high_low(v):
    high = v.astype(bf16).astype(f32)
    return high, v - high


def plane_kernel(given, gain_rows, out, rows):
    total = given[0].astype(f32)
    for i in range(1, 16):
        total += given[i].astype(f32)
    rows[...] = total
    for z in range(16):
        high, low = split_high_low(gain_rows[z : z + 1])
        out[z] = jnp.concatenate([rows[6 * z : 6 * z + 6], high, low]).astype(bf16)


def column_kernel(given, out):
    total = given[0].astype(f32)
    for z in range(1, 16):
        total += given[z].astype(f32)
    high, low = split_high_low(total[6:7] + total[7:8])
    block = jnp.concatenate([total[0:6], high, low]).astype(bf16)
    for i in range(32):
        out[i] = block


def final_kernel(given, perm, taps, proj, gain, rows):
    scale = 1.0 / 64
    for q in range(4):
        for k in range(3):
            for half in range(2):
                block = given[(q * 3 + k) * 2 + half].astype(f32)
                taps[k, 6 * q : 6 * q + 6, 384 * half : 384 * half + 384] = block[0:6] * scale
    for u in range(8):
        rows[6 * u : 6 * u + 6] = given[24 + u].astype(f32)[0:6]
    proj[...] = dot(rows[...].astype(bf16), perm[...], 1, 1) * scale
    total = given[0].astype(f32)
    for i in range(1, 32):
        total += given[i].astype(f32)
    gain[...] = ((total[6:7] + total[7:8])[:, 0:48] * scale).reshape(48)


def call(kernel, out, ins, outs, name, room, scratch=(), **more):
    return pl.pallas_call(
        kernel,
        out_shape=out,
        in_specs=ins,
        out_specs=outs,
        scratch_shapes=scratch,
        compiler_params=pltpu.CompilerParams(vmem_limit_bytes=room * MB),
        name=name,
        **more,
    )


def shape(dims, kind):
    return jax.ShapeDtypeStruct(dims, kind)


HALF = shape((16, 96, 384), bf16)
ROWS = shape((SEQS, BINS, CHANNELS), bf16)
LOCAL = pltpu.VMEM((SEQS, BINS, CHANNELS), bf16)


def waits(count):
    return pltpu.SemaphoreType.DMA((count,))


def make_piece(part, taps, proj, perm):
    return call(
        piece_kernel, shape((16, 8, 384), bf16), [SMEM] + [VMEM] * 3, VMEM, "piece", 6, [pltpu.VMEM((32, 8, 384), f32)]
    )(part, taps, proj, perm)


def make_stack(given):
    return call(stack_kernel, HALF, [VMEM], VMEM, "stack", 6, [pltpu.VMEM((96, 384), f32)])(given)


def make_norm(tokens, gain, cot):
    edge = shape((SEQS, 3 * STEP, CHANNELS), bf16)
    return call(norm_kernel, [edge, edge], [FAR] * 3, [VMEM] * 2, "norm", 6, [LOCAL, pltpu.VMEM((CHANNELS,), f32), waits(7)])(
        tokens, gain, cot
    )


def make_ready(tokens, gain, cot, perm, up, down, before, after):
    return call(
        ready_kernel,
        [
            shape((SEQS, BINS + 4 * STEP, CHANNELS), bf16),
            shape((SEQS, EXT, CHANNELS), bf16),
            shape((SEQS, BINS, CHANNELS), f32),
        ],
        [VMEM] * 8,
        [VMEM] * 3,
        "ready",
        8,
    )(tokens, gain, cot, perm, up, down, before, after)


def make_main(core, mine, other, act, cot):
    return call(
        main_kernel,
        [
            HALF,
            HALF,
            shape((SEQS, EXT, HIDDEN), bf16),
            shape((SEQS, BINS, HIDDEN), bf16),
            shape((3, HIDDEN, CHANNELS), bf16),
            shape((CHANNELS, HIDDEN), bf16),
        ],
        [SMEM] + [VMEM] * 4,
        [VMEM] * 6,
        "main",
        10,
        [pltpu.VMEM((32, 96, 384), bf16)],
    )(core, mine, other, act, cot)


def make_pair(a, b):
    return call(pair_kernel, HALF, [VMEM] * 2, VMEM, "pair", 8)(a, b)


def make_tail(taps, proj, sum_cot, hidden, slope, tokens, gain, cot, perm):
    return call(
        tail_kernel,
        [ROWS, ROWS, shape((16, 384), f32)],
        [VMEM] * 9,
        [FAR, FAR, VMEM],
        "tail",
        12,
        [pltpu.VMEM((2, SEQS, BINS, CHANNELS), bf16), waits(4)],
    )(taps, proj, sum_cot, hidden, slope, tokens, gain, cot, perm)


def make_plane(given, gain_rows):
    return call(
        plane_kernel, shape((16, 8, 384), bf16), [VMEM] * 2, VMEM, "plane", 6, [pltpu.VMEM((96, 384), f32)]
    )(given, gain_rows)


def make_column(given):
    return call(column_kernel, shape((32, 8, 384), bf16), [VMEM], VMEM, "column", 6)(given)


def make_final(given, perm):
    return call(
        final_kernel,
        [shape((3, 24, CHANNELS), f32), shape((48, 384), f32), shape((48,), f32)],
        [VMEM] * 2,
        [VMEM] * 3,
        "final",
        6,
        [pltpu.VMEM((48, 384), f32)],
    )(given, perm)


def on_device(tokens, norm_gain, dilated_weight, output_weight, cotangent):
    yx = ("y", "x")
    swap = [(0, 1), (1, 0)]
    core = lax.axis_index("c").reshape(1)
    part = core * 16 + lax.axis_index(yx)
    lane_perm = jnp.asarray(permutation(4, 16, 6), bf16)
    row_perm = jnp.asarray(permutation(8, 16, 6), bf16)

    far = [pltpu.with_memory_space_constraint(a, pltpu.HBM) for a in (tokens, norm_gain, cotangent)]
    up, down = make_norm(*far)
    before = lax.ppermute(up, "z", [(i, i + 1) for i in range(15)])
    after = lax.ppermute(down, "z", [(i + 1, i) for i in range(15)])

    piece = make_piece(part, dilated_weight.transpose(0, 2, 1), output_weight.T, lane_perm)
    from_z = lax.all_to_all(piece, "z", 0, 0)
    from_z, before, after = lax.optimization_barrier((from_z, before, after))
    mine = lax.all_to_all(make_stack(from_z), yx, 0, 0)
    mine, before, after = lax.optimization_barrier((mine, before, after))
    other = lax.ppermute(mine, "c", swap)
    act, cot_perm, slope = make_ready(tokens, norm_gain, cotangent, row_perm, up, down, before, after)

    keep, send, sum_cot, hidden, every_tap, every_proj = make_main(core, mine, other, act, cot_perm)
    received = lax.ppermute(send, "c", swap)
    residual_output, token_cotangent, gain_rows = make_tail(
        every_tap, every_proj, sum_cot, hidden, slope, tokens, norm_gain, cotangent, row_perm
    )
    received, residual_output, token_cotangent, gain_rows = lax.optimization_barrier(
        (received, residual_output, token_cotangent, gain_rows)
    )
    plane = lax.all_to_all(make_pair(keep, received), yx, 0, 0)
    column = lax.all_to_all(make_plane(plane, gain_rows), "z", 0, 0)
    spread = lax.all_to_all(make_column(column), ("c", "y", "x"), 0, 0)
    taps, proj, gain = make_final(spread, lane_perm)
    return residual_output, token_cotangent, taps.transpose(0, 2, 1), proj.T, gain


def solution(mesh):
    fine = Mesh(mesh.devices.reshape(4, 4, 2, 16), ("y", "x", "c", "z"))
    dp = ("y", "x", "c")
    rows = P(dp, "z", None)
    in_specs = (rows, P(), P(None, None, "z"), P(None, "z"), rows)
    out_specs = (rows, rows, P(None, None, "z"), P(None, "z"), P("z"))
    return jax.shard_map(on_device, mesh=fine, in_specs=in_specs, out_specs=out_specs, check_vma=False)
```

```python
import jax
import jax.numpy as jnp
import numpy as np
from jax import lax
from jax.experimental import pallas as pl
from jax.experimental.pallas import tpu as pltpu
from jax.sharding import Mesh, PartitionSpec as P

STEP = 64
SEQS = 2
BINS = 256
CHANNELS = 768
HIDDEN = 384
EXT = BINS + 2 * STEP
gelu_scale = 0.7978845608
cubic_term = 0.044715
epsilon = 1e-06
bf16 = jnp.bfloat16
f32 = jnp.float32
SMEM = pl.BlockSpec(memory_space=pltpu.SMEM)
VMEM = pl.BlockSpec(memory_space=pltpu.VMEM)
FAR = pl.BlockSpec(memory_space=pltpu.HBM)
MB = 1024 * 1024
TILE = 32


def permutation(outer, inner, width):
    size = outer * inner * width
    order = np.arange(size).reshape(inner, outer, width).transpose(1, 0, 2).reshape(-1)
    matrix = np.zeros((size, size), np.float32)
    matrix[order, np.arange(size)] = 1.0
    return matrix


def dot(a, b, ca, cb):
    return lax.dot_general(a, b, (((ca,), (cb,)), ((), ())), preferred_element_type=f32)


def tanh_of(v):
    return jnp.tanh(gelu_scale * (v + cubic_term * v * v * v))


def activate(v, t):
    return 0.5 * v * (1.0 + t)


def derivative(v, t):
    return 0.5 * (1.0 + t) + 0.5 * v * (1.0 - t * t) * gelu_scale * (1.0 + 3.0 * cubic_term * v * v)


def inverse_rms_of(v):
    return lax.rsqrt(jnp.mean(v * v, axis=-1, keepdims=True) + epsilon)


def piece_kernel(part, taps, proj, perm, out, pieces):
    for k in range(3):
        tap = taps[k].astype(f32)
        for q in range(4):
            for half in range(2):
                pieces[(q * 3 + k) * 2 + half, 0:6] = tap[6 * q : 6 * q + 6, half * 384 : half * 384 + 384]
    rows = dot(proj[...], perm[...], 1, 0)
    for u in range(8):
        pieces[24 + u, 0:6] = rows[6 * u : 6 * u + 6]
    pieces[:, 6:8] = jnp.zeros((32, 2, 384), f32)
    own = pieces[part[0]].astype(bf16)
    for z in range(16):
        out[z] = own


def stack_kernel(given, out, rows):
    for z in range(16):
        rows[6 * z : 6 * z + 6] = given[z].astype(f32)[0:6]
    packed = rows[...].astype(bf16)
    for i in range(16):
        out[i] = packed


def run(pairs, sems):
    copies = [pltpu.make_async_copy(a, b, sems.at[i]) for i, (a, b) in enumerate(pairs)]
    for c in copies:
        c.start()
    return copies


def norm_kernel(tokens, gain_in, cot, up, down, rows, gain, sems):
    loads = [(gain_in, gain)] + [(tokens.at[s], rows.at[s]) for s in range(SEQS)]
    loads += [
        (cot.at[:, BINS - STEP :], up.at[:, 2 * STEP :]),
        (cot.at[:, 0:STEP], down.at[:, 2 * STEP :]),
    ]
    loads = run(loads, sems)
    loads[0].wait()
    gain_row = gain[...].reshape(1, CHANNELS)
    for s in range(SEQS):
        loads[1 + s].wait()
        for r in range(0, BINS, TILE):
            v = rows[s, r : r + TILE].astype(f32)
            normed = v * inverse_rms_of(v) * gain_row
            edge, at = (down, r) if r < 2 * STEP else (up, r - 2 * STEP)
            edge[s, at : at + TILE] = activate(normed, tanh_of(normed)).astype(bf16)
    for c in loads[1 + SEQS :]:
        c.wait()


def ready_kernel(
    rows, gain, cots, perm, up, down, before, after,
    act, cot_perm, slope,
):
    half = 2 * STEP
    act[:, 0:half] = before[:, 0:half]
    act[:, half : 2 * half] = down[:, 0:half]
    act[:, 2 * half : 3 * half] = up[:, 0:half]
    act[:, 3 * half :] = after[:, 0:half]
    order = perm[...]
    gain_row = gain[...].reshape(1, CHANNELS)
    for s in range(SEQS):
        edges = dot(jnp.concatenate([before[s, half:], after[s, half:]]), order, 1, 0).astype(bf16)
        cot_perm[s, 0:STEP] = edges[0:STEP]
        cot_perm[s, STEP + BINS :] = edges[STEP:]
    for s in range(SEQS):
        cot_perm[s, STEP : STEP + BINS] = dot(cots[s], order, 1, 0).astype(bf16)
        for r in range(0, BINS, TILE):
            v = rows[s, r : r + TILE].astype(f32)
            normed = v * inverse_rms_of(v) * gain_row
            slope[s, r : r + TILE] = derivative(normed, tanh_of(normed))


def place(lower, upper, taps, proj):
    for p in range(32):
        piece = (lower if p < 16 else upper)[p % 16]
        if p < 24:
            q, k, half = p // 6, p % 6 // 2, p % 2
            taps[k, 96 * q : 96 * q + 96, 384 * half : 384 * half + 384] = piece
        else:
            proj[96 * (p - 24) : 96 * (p - 24) + 96] = piece


def main_kernel(
    core, mine, other, act, cot,
    keep, send, sum_cot, hidden, taps, proj,
    grad,
):
    own = BINS
    pl.when(core[0] == 0)(lambda: place(mine, other, taps, proj))
    pl.when(core[0] == 1)(lambda: place(other, mine, taps, proj))
    for s in range(SEQS):
        total = dot(act[s, 0:EXT], taps[0], 1, 1)
        total += dot(act[s, STEP : STEP + EXT], taps[1], 1, 1)
        total += dot(act[s, 2 * STEP : 2 * STEP + EXT], taps[2], 1, 1)
        hidden_cot = dot(cot[s], proj[...], 1, 0)
        for r in range(0, EXT, TILE):
            v = total[r : r + TILE]
            t = tanh_of(v)
            if STEP <= r < STEP + own:
                hidden[s, r - STEP : r - STEP + TILE] = activate(v, t).astype(bf16)
            rounded = hidden_cot[r : r + TILE].astype(bf16).astype(f32)
            sum_cot[s, r : r + TILE] = (rounded * derivative(v, t)).astype(bf16)
    centre = jnp.concatenate([sum_cot[s, STEP : STEP + own] for s in range(SEQS)])
    for k in range(3):
        rows = jnp.concatenate([act[s, STEP * (k + 1) : STEP * (k + 1) + own] for s in range(SEQS)])
        g = dot(centre, rows, 0, 0).astype(bf16)
        for q in range(4):
            for half in range(2):
                grad[(q * 3 + k) * 2 + half] = g[96 * q : 96 * q + 96, 384 * half : 384 * half + 384]
    rows = jnp.concatenate([cot[s, STEP : STEP + own] for s in range(SEQS)])
    g = dot(rows, jnp.concatenate([hidden[s] for s in range(SEQS)]), 0, 0).astype(bf16)
    for u in range(8):
        grad[24 + u] = g[96 * u : 96 * u + 96]

    @pl.when(core[0] == 0)
    def _():
        keep[...] = grad[0:16]
        send[...] = grad[16:32]

    @pl.when(core[0] == 1)
    def _():
        keep[...] = grad[16:32]
        send[...] = grad[0:16]


def pair_kernel(a, b, out):
    out[...] = (a[...].astype(f32) + b[...].astype(f32)).astype(bf16)


def tail_kernel(
    taps, proj, sum_cot, hidden, slope, rows, gain, cots, perm,
    block_output, token_gradient, gain_rows,
    result, out_sems,
):
    gain_row = gain[...].reshape(1, CHANNELS)
    gain_sum = jnp.zeros((1, CHANNELS), f32)
    saves = []
    for s in range(SEQS):
        total = dot(sum_cot[s, 2 * STEP : 2 * STEP + BINS], taps[0], 1, 0)
        total += dot(sum_cot[s, STEP : STEP + BINS], taps[1], 1, 0)
        total += dot(sum_cot[s, 0:BINS], taps[2], 1, 0)
        for r in range(0, BINS, TILE):
            at = slice(r, r + TILE)
            v = rows[s, at].astype(f32)
            normed_cot = total[at].astype(bf16).astype(f32) * slope[s, at]
            inverse_rms = inverse_rms_of(v)
            scaled_cot = gain_row * normed_cot
            mean = jnp.mean(scaled_cot * v, axis=-1, keepdims=True)
            result[1, s, at] = (
                cots[s, at].astype(f32) + inverse_rms * scaled_cot - v * (inverse_rms * inverse_rms * inverse_rms) * mean
            ).astype(bf16)
            gain_sum += jnp.sum(normed_cot * v * inverse_rms, axis=0, keepdims=True)
        saves.append(pltpu.make_async_copy(result.at[1, s], token_gradient.at[s], out_sems.at[2 * s + 1]))
        saves[-1].start()
    natural = dot(proj[...], perm[...], 0, 1).astype(bf16)
    for s in range(SEQS):
        result[0, s] = (rows[s].astype(f32) + dot(hidden[s], natural, 1, 0)).astype(bf16)
        saves.append(pltpu.make_async_copy(result.at[0, s], block_output.at[s], out_sems.at[2 * s]))
        saves[-1].start()
    gain_rows[...] = jnp.zeros((16, 384), f32)
    for z in range(16):
        gain_rows[z : z + 1, 0:48] = gain_sum[:, 48 * z : 48 * z + 48]
    for c in saves:
        c.wait()


def split_high_low(v):
    high = v.astype(bf16).astype(f32)
    return high, v - high


def plane_kernel(given, gain_rows, out, rows):
    total = given[0].astype(f32)
    for i in range(1, 16):
        total += given[i].astype(f32)
    rows[...] = total
    for z in range(16):
        high, low = split_high_low(gain_rows[z : z + 1])
        out[z] = jnp.concatenate([rows[6 * z : 6 * z + 6], high, low]).astype(bf16)


def column_kernel(given, out):
    total = given[0].astype(f32)
    for z in range(1, 16):
        total += given[z].astype(f32)
    high, low = split_high_low(total[6:7] + total[7:8])
    block = jnp.concatenate([total[0:6], high, low]).astype(bf16)
    for i in range(32):
        out[i] = block


def final_kernel(given, perm, taps, proj, gain, rows):
    scale = 1.0 / 64
    for q in range(4):
        for k in range(3):
            for half in range(2):
                block = given[(q * 3 + k) * 2 + half].astype(f32)
                taps[k, 6 * q : 6 * q + 6, 384 * half : 384 * half + 384] = block[0:6] * scale
    for u in range(8):
        rows[6 * u : 6 * u + 6] = given[24 + u].astype(f32)[0:6]
    proj[...] = dot(rows[...].astype(bf16), perm[...], 1, 1) * scale
    total = given[0].astype(f32)
    for i in range(1, 32):
        total += given[i].astype(f32)
    gain[...] = ((total[6:7] + total[7:8])[:, 0:48] * scale).reshape(48)


def call(kernel, out, ins, outs, name, room, scratch=(), **more):
    return pl.pallas_call(
        kernel,
        out_shape=out,
        in_specs=ins,
        out_specs=outs,
        scratch_shapes=scratch,
        compiler_params=pltpu.CompilerParams(vmem_limit_bytes=room * MB),
        name=name,
        **more,
    )


def shape(dims, kind):
    return jax.ShapeDtypeStruct(dims, kind)


HALF = shape((16, 96, 384), bf16)
ROWS = shape((SEQS, BINS, CHANNELS), bf16)
LOCAL = pltpu.VMEM((SEQS, BINS, CHANNELS), bf16)


def waits(count):
    return pltpu.SemaphoreType.DMA((count,))


def make_piece(part, taps, proj, perm):
    return call(
        piece_kernel, shape((16, 8, 384), bf16), [SMEM] + [VMEM] * 3, VMEM, "piece", 6, [pltpu.VMEM((32, 8, 384), f32)]
    )(part, taps, proj, perm)


def make_stack(given):
    return call(stack_kernel, HALF, [VMEM], VMEM, "stack", 6, [pltpu.VMEM((96, 384), f32)])(given)


def make_norm(tokens, gain, cot):
    edge = shape((SEQS, 3 * STEP, CHANNELS), bf16)
    return call(norm_kernel, [edge, edge], [FAR] * 3, [VMEM] * 2, "norm", 6, [LOCAL, pltpu.VMEM((CHANNELS,), f32), waits(5)])(
        tokens, gain, cot
    )


def make_ready(tokens, gain, cot, perm, up, down, before, after):
    return call(
        ready_kernel,
        [
            shape((SEQS, BINS + 4 * STEP, CHANNELS), bf16),
            shape((SEQS, EXT, CHANNELS), bf16),
            shape((SEQS, BINS, CHANNELS), f32),
        ],
        [VMEM] * 8,
        [VMEM] * 3,
        "ready",
        8,
    )(tokens, gain, cot, perm, up, down, before, after)


def make_main(core, mine, other, act, cot):
    return call(
        main_kernel,
        [
            HALF,
            HALF,
            shape((SEQS, EXT, HIDDEN), bf16),
            shape((SEQS, BINS, HIDDEN), bf16),
            shape((3, HIDDEN, CHANNELS), bf16),
            shape((CHANNELS, HIDDEN), bf16),
        ],
        [SMEM] + [VMEM] * 4,
        [VMEM] * 6,
        "main",
        10,
        [pltpu.VMEM((32, 96, 384), bf16)],
    )(core, mine, other, act, cot)


def make_pair(a, b):
    return call(pair_kernel, HALF, [VMEM] * 2, VMEM, "pair", 8)(a, b)


def make_tail(taps, proj, sum_cot, hidden, slope, tokens, gain, cot, perm):
    return call(
        tail_kernel,
        [ROWS, ROWS, shape((16, 384), f32)],
        [VMEM] * 9,
        [FAR, FAR, VMEM],
        "tail",
        12,
        [pltpu.VMEM((2, SEQS, BINS, CHANNELS), bf16), waits(4)],
    )(taps, proj, sum_cot, hidden, slope, tokens, gain, cot, perm)


def make_plane(given, gain_rows):
    return call(
        plane_kernel, shape((16, 8, 384), bf16), [VMEM] * 2, VMEM, "plane", 6, [pltpu.VMEM((96, 384), f32)]
    )(given, gain_rows)


def make_column(given):
    return call(column_kernel, shape((32, 8, 384), bf16), [VMEM], VMEM, "column", 6)(given)


def make_final(given, perm):
    return call(
        final_kernel,
        [shape((3, 24, CHANNELS), f32), shape((48, 384), f32), shape((48,), f32)],
        [VMEM] * 2,
        [VMEM] * 3,
        "final",
        6,
        [pltpu.VMEM((48, 384), f32)],
    )(given, perm)


def on_device(tokens, norm_gain, dilated_weight, output_weight, cotangent):
    yx = ("y", "x")
    swap = [(0, 1), (1, 0)]
    core = lax.axis_index("c").reshape(1)
    part = core * 16 + lax.axis_index(yx)
    lane_perm = jnp.asarray(permutation(4, 16, 6), bf16)
    row_perm = jnp.asarray(permutation(8, 16, 6), bf16)

    far = [pltpu.with_memory_space_constraint(a, pltpu.HBM) for a in (tokens, norm_gain, cotangent)]
    up, down = make_norm(*far)
    before = lax.ppermute(up, "z", [(i, i + 1) for i in range(15)])
    after = lax.ppermute(down, "z", [(i + 1, i) for i in range(15)])

    piece = make_piece(part, dilated_weight.transpose(0, 2, 1), output_weight.T, lane_perm)
    from_z = lax.all_to_all(piece, "z", 0, 0)
    from_z, before, after = lax.optimization_barrier((from_z, before, after))
    mine = lax.all_to_all(make_stack(from_z), yx, 0, 0)
    mine, before, after = lax.optimization_barrier((mine, before, after))
    other = lax.ppermute(mine, "c", swap)
    act, cot_perm, slope = make_ready(tokens, norm_gain, cotangent, row_perm, up, down, before, after)

    keep, send, sum_cot, hidden, every_tap, every_proj = make_main(core, mine, other, act, cot_perm)
    received = lax.ppermute(send, "c", swap)
    residual_output, token_cotangent, gain_rows = make_tail(
        every_tap, every_proj, sum_cot, hidden, slope, tokens, norm_gain, cotangent, row_perm
    )
    received, residual_output, token_cotangent, gain_rows = lax.optimization_barrier(
        (received, residual_output, token_cotangent, gain_rows)
    )
    plane = lax.all_to_all(make_pair(keep, received), yx, 0, 0)
    column = lax.all_to_all(make_plane(plane, gain_rows), "z", 0, 0)
    spread = lax.all_to_all(make_column(column), ("c", "y", "x"), 0, 0)
    taps, proj, gain = make_final(spread, lane_perm)
    return residual_output, token_cotangent, taps.transpose(0, 2, 1), proj.T, gain


def solution(mesh):
    fine = Mesh(mesh.devices.reshape(4, 4, 2, 16), ("y", "x", "c", "z"))
    dp = ("y", "x", "c")
    rows = P(dp, "z", None)
    in_specs = (rows, P(), P(None, None, "z"), P(None, "z"), rows)
    out_specs = (rows, rows, P(None, None, "z"), P(None, "z"), P("z"))
    return jax.shard_map(on_device, mesh=fine, in_specs=in_specs, out_specs=out_specs, check_vma=False)
```
